128 devices in a mesh: dp: 64 (over x, z, y), mp: 2 (over core).
Axes of the slice: x: 4, y: 4, z: 4, core: 2. Of those that a mesh axis runs over, the one named last changes fastest.
Arguments:
- features: bfloat16 [32768, 2048], P('dp', 'mp'), may hold values from -6 to 6
- gains: float32 [2, 2048], replicated, may hold values from 0.25 to 1.75
- weights: bfloat16 [2, 2048, 2048], P(None, None, 'mp'), may hold values from -0.125 to 0.125
- heads: bfloat16 [4096, 32, 2048], P('dp', None, 'mp'), may hold values from -0.125 to 0.125
- lengths: int32 [64, 64], P('dp'), may hold values from 1 to 8, 256 in all within a row
- owners: int32 [64, 64], P('dp'), may hold values from 0 to 63, each once within a row
- labels: int32 [32768], P('dp'), may hold values from 0 to 31
Outputs:
- body_grads: float32 [2, 2048, 2048], P(None, 'dp', 'mp')
- token_loss: bfloat16 [32768], P('dp')
The draws below stay inside these ranges and needn't reach their ends.
Inputs may be any that keep to these rules, and one draw needn't show every extreme that they name: `lengths`: each row (one block's 64 clients) holds token counts of 1 to 8 that sum to 256; some client of each block holds exactly 8. `owners`: each row names every head owner 0 to 63 exactly once.
All inputs are finite; a program needn't handle non-finite values.
Results may differ from the reference program's by a relative error of at most 0.0073.
Values may be sent and summed in bfloat16 or wider, within the bound.
A program may use at most 128 MiB of HBM per device.

```python
import math
import jax
import jax.numpy as jnp
import numpy as np
from jax import lax

D = 2048
CLASSES = 32
TOK_DEV = 512
MOST = 8
CLIENTS = 4096
TOKENS = 32768
N_DP = 64


def place_ends(array, key, least, top_value):
    longest = array.shape.index(max(array.shape))
    spots = []
    for shift in (0, 1):
        where = [jax.random.randint(jax.random.fold_in(key, axis), (), 0, length) for axis, length in enumerate(array.shape)]
        where[longest] = (where[longest] + shift) % array.shape[longest]
        spots.append(tuple(where))
    return array.at[spots[0]].set(least).at[spots[1]].set(top_value)


def steps_of(stream_key, dims, pieces, least, largest):
    gain = 1.0
    for position, shards_of in pieces:
        heights = jax.random.uniform(jax.random.fold_in(jax.random.fold_in(stream_key, 6), position), (shards_of,), jnp.float32, least / len(pieces), largest / len(pieces))
        gain = gain * jnp.repeat(jnp.exp(heights), dims[position] // shards_of).reshape((-1,) + (1,) * (len(dims) - 1 - position))
    return gain


def length_profile(number_of, total, limit, skew):
    loads = [(1 << 20) // math.isqrt(rank ** skew) + 1 for rank in range(2, number_of + 1)]
    rest, given = total - limit - (number_of - 1), [1] * (number_of - 1)
    while rest > 0:
        free = [i for i in range(number_of - 1) if given[i] < limit]
        whole, remaining = sum([loads[i] for i in free]), rest
        for i in free:
            more = min(limit - given[i], max(1, remaining * loads[i] // whole), rest)
            given[i] = given[i] + more
            rest = rest - more
    return np.array([limit] + given)


def uneven_parts(key, count, total, reach, lean):
    if count == 2:
        one = jax.random.randint(key, (), max(1, total - reach), min(reach, total - 1) + 1)
        return jnp.stack([one, total - one])
    sizes = jnp.asarray(length_profile(count, total, reach, lean), jnp.int32)
    twos = (count - 1) // 2
    donor, receiver = sizes[1:1 + 2 * twos:2], sizes[2:2 + 2 * twos:2]
    slack = jnp.minimum(donor - 1, reach - receiver)
    passed = jax.random.randint(jax.random.fold_in(key, 1), (twos,), 0, 1 << 20) % (slack + 1)
    sizes = sizes.at[1:1 + 2 * twos:2].set(donor - passed).at[2:2 + 2 * twos:2].set(receiver + passed)
    return sizes[jax.random.permutation(jax.random.fold_in(key, 2), count)]


def centred(key, extent, width, bound, shards=(), kind=jnp.bfloat16):
    factor_of = steps_of(key, extent, shards, -0.22, 0.18) if shards else 1.0
    values = jax.random.normal(key, extent, jnp.float32) * width * factor_of
    return jnp.minimum(jnp.maximum(values, -bound), bound).astype(kind)


def setup_inputs(seed: int = 0) -> dict:
    arg_keys = jax.random.split(jax.random.key(seed), 8)
    return {
        "features": centred(arg_keys[0], (TOKENS, D), 1.0, 6.0, ((0, 64), (1, 2))),
        "gains": jnp.clip(1.0 + 0.15 * jax.random.normal(arg_keys[1], (2, D), jnp.float32), 0.25, 1.75),
        "weights": centred(arg_keys[2], (2, D, D), D ** -0.5, 0.125, ((2, 2),)),
        "heads": centred(arg_keys[3], (CLIENTS, CLASSES, D), D ** -0.5, 0.125, ((0, 64), (2, 2))),
        "lengths": jax.vmap(lambda own: uneven_parts(own, N_DP, TOK_DEV // 2, MOST, 2))(jax.random.split(arg_keys[4], N_DP)).reshape((N_DP, N_DP)).astype(jnp.int32),
        "owners": jax.vmap(lambda own: jax.random.permutation(own, N_DP))(jax.random.split(arg_keys[5], N_DP)).reshape((N_DP, N_DP)).astype(jnp.int32),
        "labels": place_ends(jax.random.randint(arg_keys[6], (TOKENS,), 0, CLASSES), jax.random.fold_in(arg_keys[6], 1), 0, CLASSES - 1).astype(jnp.int32),
    }


EPSILON = 1e-06

def norm_layer(inputs, norm_gain, weight):
    widened = inputs.astype(jnp.float32)
    rms_scale = lax.rsqrt(lax.optimization_barrier(jnp.mean(widened * widened, -1, keepdims=True)) + EPSILON)
    normed = (widened * rms_scale * norm_gain).astype(jnp.bfloat16)
    pre_act = jnp.dot(normed, weight, preferred_element_type=jnp.float32)
    outputs = (widened + jax.nn.gelu(pre_act)).astype(jnp.bfloat16)
    return (normed, rms_scale, pre_act, outputs)

def gelu_back(pre_act, upstream):
    return jax.vjp(jax.nn.gelu, pre_act)[1](upstream)[0]

def loss_terms(logits, slot_labels, slot_lens):
    class_ids = lax.broadcasted_iota(jnp.int32, logits.shape, 2)
    class_hit = class_ids == slot_labels[..., None]
    log_total = jnp.log(lax.optimization_barrier(jnp.sum(jnp.exp(logits), -1)))
    picked = lax.optimization_barrier(jnp.sum(jnp.where(class_hit, logits, 0.0), -1))
    slot_live = slot_lens > 0
    losses = jnp.where(slot_live, log_total - picked, 0.0)
    weight_tok = jnp.where(slot_live, 1.0 / jnp.maximum(slot_lens, 1).astype(logits.dtype), 0.0)
    softmax_probs = jnp.exp(logits - log_total[..., None])
    dlogits = ((softmax_probs - class_hit.astype(logits.dtype)) * weight_tok[..., None]).astype(jnp.bfloat16)
    return (losses.astype(jnp.bfloat16), dlogits)

def reference(features, gains, weights, heads, lengths, owners, labels):
    normed_first, scale_first, pre_first, hidden_mid = norm_layer(features, gains[0], weights[0])
    normed_second, scale_second, pre_second, hidden_top = norm_layer(hidden_mid, gains[1], weights[1])
    heads_grid = heads.reshape(N_DP, N_DP, CLASSES, D)

    def device_heads(device_item):
        slot_source, dev_labels, dev_lengths, dev_owners, source = device_item
        client_ends = jnp.cumsum(dev_lengths).astype(jnp.int32)
        starts = (client_ends - dev_lengths).astype(jnp.int32)
        offsets = jnp.arange(MOST, dtype=jnp.int32)
        slot_live = offsets[None, :] < dev_lengths[:, None]
        slot_index = jnp.where(slot_live, starts[:, None] + offsets[None, :], TOK_DEV).reshape(-1).astype(jnp.int32)
        safe_index = jnp.minimum(slot_index, TOK_DEV - 1).astype(jnp.int32)
        slot_feats = slot_source[safe_index].reshape(N_DP, MOST, D).astype(jnp.float32)
        slot_heads = heads_grid[dev_owners, source].astype(jnp.float32)
        logits = jnp.einsum('jmd,jcd->jmc', slot_feats, slot_heads)
        slot_labels = dev_labels[safe_index].reshape(N_DP, MOST)
        slot_lens = jnp.where(slot_live, dev_lengths[:, None], 0)
        losses, dlogits = loss_terms(logits, slot_labels, slot_lens)
        slot_grads = jnp.einsum('jmc,jcd->jmd', dlogits.astype(jnp.float32), slot_heads).astype(jnp.bfloat16)
        tok_grads = jnp.zeros((TOK_DEV, D), jnp.bfloat16).at[slot_index].add(slot_grads.reshape(-1, D), mode='drop')
        tok_loss = jnp.zeros((TOK_DEV,), jnp.bfloat16).at[slot_index].add(losses.reshape(-1), mode='drop')
        return (tok_grads, tok_loss)
    tok_grads, tok_loss = lax.map(device_heads, (hidden_top.reshape(N_DP, TOK_DEV, D), labels.reshape(N_DP, TOK_DEV), lengths, owners, jnp.arange(N_DP, dtype=jnp.int32)))
    upstream = tok_grads.reshape(TOKENS, D).astype(jnp.float32)
    delta_second = gelu_back(pre_second, upstream).astype(jnp.bfloat16)
    grad_second = lax.dot_general(normed_second, delta_second, (((0,), (0,)), ((), ())), preferred_element_type=jnp.float32)
    dnormed = jnp.dot(delta_second, weights[1].T, preferred_element_type=jnp.float32)
    widened = hidden_mid.astype(jnp.float32)
    cross_term = lax.optimization_barrier(jnp.mean(widened * gains[1] * dnormed, -1, keepdims=True))
    dhidden = upstream + gains[1] * scale_second * dnormed - widened * scale_second ** 3 * cross_term
    delta_first = gelu_back(pre_first, dhidden).astype(jnp.bfloat16)
    grad_first = lax.dot_general(normed_first, delta_first, (((0,), (0,)), ((), ())), preferred_element_type=jnp.float32)
    return (jnp.stack([grad_first, grad_second]), tok_loss.reshape(TOKENS))
```

```python
import functools

import jax
import jax.numpy as jnp
from jax import lax
from jax.experimental import pallas as pl
from jax.experimental.pallas import tpu as pltpu
from jax.sharding import PartitionSpec as P

EPSILON = 1e-06
MESH = pl.DeviceIdType.MESH
STRIDES = (16, 4, 1)
WIDTHS = ((384, 256, 384), (384, 384, 256))
STARTS = tuple(tuple(sum(w[:k]) for k in range(3)) for w in WIDTHS)
UNITS = (32, 8, 2)

def blend(core, a, b):
    return a + core * (b - a)

class Ring:
    def __init__(self, me, core, bufs):
        self.me, self.core = me, core
        self.g, self.t1, self.t2, self.rx, self.tx, self.ssem, self.rsem = bufs
        self.coords = tuple((me // s) % 4 for s in STRIDES)

    def dim(self, c, ph):
        k0, k1 = (c + ph) % 3, (c + ph + 1) % 3
        stride = blend(self.core, STRIDES[k0], STRIDES[k1])
        p = blend(self.core, self.coords[k0], self.coords[k1])
        right = self.me + ((p + 1) % 4 - p) * stride
        left = self.me + ((p + 3) % 4 - p) * stride
        return p, right, left

    def src(self, l, c, ph):
        return (self.g, self.t1, self.t2)[ph][l * 3 + c]

    def copy(self, l, c, ph, k, src, to):
        n = l * 3 + c
        return pltpu.make_async_remote_copy(
            src_ref=src, dst_ref=self.rx[ph][n].at[k],
            send_sem=self.ssem.at[n, ph, k], recv_sem=self.rsem.at[n, ph, k],
            device_id=(to, self.core), device_id_type=MESH)

    def copies(self, l, c, ph):
        p, right, left = self.dim(c, ph)
        P, H, tx = self.src(l, c, ph), UNITS[ph] // 2, self.tx[ph][l * 3 + c]
        half = (pl.ds(0, H), pl.ds(H, H))
        def nth(k):
            if k < 4:
                src = P.at[(p + (2, 1, 2, 3)[k]) % 4, half[(0, 1, 1, 0)[k]]]
            else:
                src = tx.at[k - 4]
            return self.copy(l, c, ph, k, src, (right, right, left, left, right, left)[k])
        return nth

    def start_a(self, l, c, ph):
        cp = self.copies(l, c, ph)
        for k in (0, 2, 1, 3):
            cp(k).start()

    def step_b(self, l, c, ph):
        cp = self.copies(l, c, ph)
        p, _, _ = self.dim(c, ph)
        P, H = self.src(l, c, ph), UNITS[ph] // 2
        rx, tx = self.rx[ph][l * 3 + c], self.tx[ph][l * 3 + c]
        for k, q, off in ((0, (p + 1) % 4, 0), (2, (p + 3) % 4, H)):
            cp(k).wait_recv()
            def add(u, n):
                tx[k // 2, pl.ds(u, n)] = (P[q, pl.ds(off + u, n)].astype(jnp.float32) + rx[k, pl.ds(u, n)].astype(jnp.float32)).astype(jnp.bfloat16)
            self.each(H, add)
            cp(4 + k // 2).start()

    def finish(self, l, c, ph, store):
        cp = self.copies(l, c, ph)
        p, _, _ = self.dim(c, ph)
        P, H = self.src(l, c, ph), UNITS[ph] // 2
        rx = self.rx[ph][l * 3 + c]
        for a, b, off in ((3, 4, 0), (1, 5, H)):
            cp(a).wait_recv()
            cp(b).wait_recv()
            def add(u, n):
                store(off + u, n, P[p, pl.ds(off + u, n)].astype(jnp.float32) + rx[a, pl.ds(u, n)].astype(jnp.float32) + rx[b, pl.ds(u, n)].astype(jnp.float32))
            self.each(H, add)

    @staticmethod
    def each(count, f):
        n = min(count, 4)
        if count == n:
            f(0, n)
        else:
            def body(i, c):
                f(pl.multiple_of(i * n, n), n)
                return c
            lax.fori_loop(0, count // n, body, 0)

    def next_phase(self, l, c, ph):
        t = (self.t1, self.t2)[ph][l * 3 + c]
        per = UNITS[ph + 1]
        def store(u, n, v):
            m = min(n, per)
            for j in range(0, n, m):
                q, r = (u + j) // per, (u + j) % per
                t[q, pl.ds(r, m)] = v[j:j + m].astype(jnp.bfloat16)
        self.finish(l, c, ph, store)
        self.start_a(l, c, ph + 1)

    def last(self, l, c, out):
        w0, w = STARTS[l][c], WIDTHS[l][c]
        def store(u, n, v):
            for j in range(n):
                out[l, (u + j) * 16:(u + j + 1) * 16, w0:w0 + w] = v[j]
        self.finish(l, c, 2, store)

    def put_partial(self, l, x, z, y, val):
        xyz = (x, z, y)
        v = val.astype(jnp.bfloat16).reshape(2, 16, 1024)
        for c in range(3):
            a, b, d = (blend(self.core, xyz[(c + k) % 3], xyz[(c + k + 1) % 3]) for k in range(3))
            w0, w = STARTS[l][c], WIDTHS[l][c]
            self.g[l * 3 + c][a, pl.ds((b * 4 + d) * 2, 2)] = v[:, :, w0:w0 + w]

    def wait_sends(self):
        for l in range(2):
            for c in range(3):
                for ph in range(3):
                    for k in range(6):
                        self.copies(l, c, ph)(k).wait_send()

def scratch():
    lc = [(l, c) for l in range(2) for c in range(3)]
    bf = jnp.bfloat16
    return [
        [pltpu.VMEM((4, 32, 16, WIDTHS[l][c]), bf) for l, c in lc],
        [pltpu.VMEM((4, 8, 16, WIDTHS[l][c]), bf) for l, c in lc],
        [pltpu.VMEM((4, 2, 16, WIDTHS[l][c]), bf) for l, c in lc],
        [[pltpu.VMEM((6, n // 2, 16, WIDTHS[l][c]), bf) for l, c in lc] for n in UNITS],
        [[pltpu.VMEM((2, n // 2, 16, WIDTHS[l][c]), bf) for l, c in lc] for n in UNITS],
        pltpu.SemaphoreType.DMA((6, 3, 6)),
        pltpu.SemaphoreType.DMA((6, 3, 6)),
    ]

def flat(tree):
    return jax.tree.flatten(tree, is_leaf=lambda v: not isinstance(v, list))

def enter(me, core):
    bar = pltpu.get_barrier_semaphore()
    for s in STRIDES:
        p = (me // s) % 4
        for step in (1, 3):
            pl.semaphore_signal(bar, inc=1, device_id=(me + ((p + step) % 4 - p) * s, core), device_id_type=MESH)
    pl.semaphore_wait(bar, 6)

def partials(ring, l, nt_ref, delta_ref):
    def group(x, carry):
        rows = pl.ds(pl.multiple_of(x * 512, 512), 512)
        prod = jnp.dot(nt_ref[l, rows, :], delta_ref[l], preferred_element_type=jnp.float32)
        for z in range(4):
            for y in range(4):
                b = (z * 4 + y) * 32
                ring.put_partial(l, x, z, y, prod[b:b + 32])
        return carry
    lax.fori_loop(0, 4, group, 0)

def rs_kernel(tree, nt_ref, delta_ref, out, *refs):
    me, core = lax.axis_index("dp"), lax.axis_index("mp")
    ring = Ring(me, core, jax.tree.unflatten(tree, refs))
    enter(me, core)
    order = (1, 0)
    for l in order:
        partials(ring, l, nt_ref, delta_ref)
        for c in range(3):
            ring.start_a(l, c, 0)
    for ph in range(3):
        for l in order:
            for c in range(3):
                ring.step_b(l, c, ph)
        for l in order:
            for c in range(3):
                if ph < 2:
                    ring.next_phase(l, c, ph)
                else:
                    ring.last(l, c, out)
    ring.wait_sends()

def rs_call(nt, delta, cid=0):
    leaves, tree = flat(scratch())
    return pl.pallas_call(functools.partial(rs_kernel, tree),
        out_shape=jax.ShapeDtypeStruct((2, 32, 1024), jnp.float32),
        in_specs=[pl.BlockSpec(memory_space=pltpu.VMEM)] * 2,
        out_specs=pl.BlockSpec(memory_space=pltpu.VMEM),
        scratch_shapes=leaves,
        compiler_params=pltpu.CompilerParams(collective_id=cid, has_side_effects=True, vmem_limit_bytes=56 << 20),
        name="grad_rs")(nt, delta)


def sent_to_all(value, axis):
    devices = lax.axis_size(axis)
    return lax.all_to_all(
        jnp.broadcast_to(value[None], (devices, *value.shape)), axis, 0, 0, tiled=True
    )


def widen_rows(narrow):
    tiles = jnp.moveaxis(sent_to_all(narrow, "mp"), 0, 1)
    return tiles.reshape(narrow.shape[0], -1)


def of_everyone(value, axis):
    return sent_to_all(value, axis).sum(axis=0)


def sum_at_owner(value, axis):
    rows, cols = value.shape
    devices = lax.axis_size(axis)
    tiles = jnp.moveaxis(value.reshape(rows, devices, cols // devices), 1, 0)
    arrived = lax.all_to_all(tiles, axis, split_axis=0, concat_axis=0, tiled=True)
    return arrived.astype(jnp.float32).sum(axis=0)


def gelu_back(pre_act, upstream):
    return jax.vjp(jax.nn.gelu, pre_act)[1](upstream)[0]


def norm_layer(full_rows, own_cols, norm_gain, weight):
    widened = full_rows.astype(jnp.float32)
    rms_scale = lax.rsqrt(jnp.mean(widened * widened, -1, keepdims=True) + EPSILON)
    normed = (widened * rms_scale * norm_gain).astype(jnp.bfloat16)
    pre_act = jnp.dot(normed, weight, preferred_element_type=jnp.float32)
    outputs = (own_cols.astype(jnp.float32) + jax.nn.gelu(pre_act)).astype(jnp.bfloat16)
    return (normed, rms_scale, pre_act, outputs)


def body(features, gains, weights, heads, lengths, owners, labels):
    slots, half_width = features.shape
    groups = lax.axis_size("dp")
    classes = heads.shape[1]
    live = slots // 2
    block_heads = lax.all_to_all(heads, "dp", 0, 0, tiled=True)
    own_first = features[:live]
    rows_first = widen_rows(own_first)
    full_width = rows_first.shape[1]
    normed_first, scale_first, pre_first, hidden_mid = norm_layer(
        rows_first, own_first, gains[0], weights[0]
    )
    rows_second = widen_rows(hidden_mid)
    normed_second, scale_second, pre_second, hidden_top = norm_layer(
        rows_second, hidden_mid, gains[1], weights[1]
    )
    ends = jnp.cumsum(lengths[0])
    slot = lax.broadcasted_iota(jnp.int32, (groups, live), 1)
    here = (slot < ends[:, None]) & (slot >= (ends - lengths[0])[:, None])
    slot_owner = jnp.sum(jnp.where(here, owners[0][:, None], 0), 0)
    slot_len = jnp.sum(jnp.where(here, lengths[0][:, None], 0), 0)
    mine = lax.broadcasted_iota(jnp.int32, (groups, live), 0) == slot_owner[None, :]
    all_logits = lax.dot_general(
        block_heads, hidden_top, (((2,), (1,)), ((), ())), preferred_element_type=jnp.float32
    )
    part = jnp.sum(jnp.where(mine[:, None, :], all_logits, 0.0), 0)
    logits = of_everyone(part, "mp")
    hit = lax.broadcasted_iota(jnp.int32, (classes, live), 0) == labels[:live][None, :]
    log_total = jnp.log(jnp.sum(jnp.exp(logits), 0))
    losses = (log_total - jnp.sum(jnp.where(hit, logits, 0.0), 0)).astype(jnp.bfloat16)
    dlogits = (
        (jnp.exp(logits - log_total[None]) - hit.astype(jnp.float32))
        * (1.0 / slot_len.astype(jnp.float32))[None]
    ).astype(jnp.bfloat16)
    spread = jnp.where(mine[:, None, :], dlogits[None], jnp.zeros((), jnp.bfloat16))
    upstream = (
        lax.dot_general(
            spread, block_heads, (((0, 1), (0, 1)), ((), ())), preferred_element_type=jnp.float32
        )
        .astype(jnp.bfloat16)
        .astype(jnp.float32)
    )
    delta_second = gelu_back(pre_second, upstream).astype(jnp.bfloat16)
    dnormed_part = lax.dot_general(
        delta_second, weights[1], (((1,), (1,)), ((), ())), preferred_element_type=jnp.float32
    )
    gain_cols = lax.dynamic_slice_in_dim(gains[1], lax.axis_index("mp") * half_width, half_width, 0)
    hidden_cols = hidden_mid.astype(jnp.float32)
    dnormed = sum_at_owner(dnormed_part.astype(jnp.bfloat16), "mp")
    cross_term = of_everyone(jnp.sum(hidden_cols * gain_cols * dnormed, -1), "mp") / full_width
    dhidden = (
        upstream
        + gain_cols * scale_second * dnormed
        - hidden_cols * scale_second**3 * cross_term[:, None]
    )
    delta_first = gelu_back(pre_first, dhidden).astype(jnp.bfloat16)
    grads = rs_call(
        jnp.stack([normed_first.T, normed_second.T]), jnp.stack([delta_first, delta_second])
    )
    return (grads, jnp.concatenate([losses, jnp.zeros((slots - live,), jnp.bfloat16)]))


def solution(mesh):
    return jax.shard_map(
        body,
        mesh=mesh,
        in_specs=(
            P("dp", "mp"),
            P(),
            P(None, None, "mp"),
            P("dp", None, "mp"),
            P("dp", None),
            P("dp", None),
            P("dp"),
        ),
        out_specs=(P(None, "dp", "mp"), P("dp")),
        check_vma=False,
    )
```

```python
import functools
import math

import jax
import jax.numpy as jnp
from jax import lax
from jax.experimental import pallas as pl
from jax.experimental.pallas import tpu as pltpu
from jax.sharding import PartitionSpec as P

EPSILON = 1e-06
MESH = pl.DeviceIdType.MESH
STRIDES = (16, 4, 1)
WIDTHS = ((384, 256, 384), (384, 384, 256))
STARTS = tuple(tuple(sum(w[:k]) for k in range(3)) for w in WIDTHS)
UNITS = (32, 8, 2)

def blend(core, a, b):
    return a + core * (b - a)

class Ring:
    def __init__(self, me, core, bufs):
        self.me, self.core = me, core
        self.g, self.t1, self.t2, self.rx, self.tx, self.ssem, self.rsem = bufs
        self.coords = tuple((me // s) % 4 for s in STRIDES)

    def dim(self, c, ph):
        k0, k1 = (c + ph) % 3, (c + ph + 1) % 3
        stride = blend(self.core, STRIDES[k0], STRIDES[k1])
        p = blend(self.core, self.coords[k0], self.coords[k1])
        right = self.me + ((p + 1) % 4 - p) * stride
        left = self.me + ((p + 3) % 4 - p) * stride
        return p, right, left

    def src(self, l, c, ph):
        return (self.g, self.t1, self.t2)[ph][l * 3 + c]

    def copy(self, l, c, ph, k, src, to):
        n = l * 3 + c
        return pltpu.make_async_remote_copy(
            src_ref=src, dst_ref=self.rx[ph][n].at[k],
            send_sem=self.ssem.at[n, ph, k], recv_sem=self.rsem.at[n, ph, k],
            device_id=(to, self.core), device_id_type=MESH)

    def copies(self, l, c, ph):
        p, right, left = self.dim(c, ph)
        P, H, tx = self.src(l, c, ph), UNITS[ph] // 2, self.tx[ph][l * 3 + c]
        half = (pl.ds(0, H), pl.ds(H, H))
        def nth(k):
            if k < 4:
                src = P.at[(p + (2, 1, 2, 3)[k]) % 4, half[(0, 1, 1, 0)[k]]]
            else:
                src = tx.at[k - 4]
            return self.copy(l, c, ph, k, src, (right, right, left, left, right, left)[k])
        return nth

    def start_a(self, l, c, ph):
        cp = self.copies(l, c, ph)
        for k in (0, 2, 1, 3):
            cp(k).start()

    def step_b(self, l, c, ph):
        cp = self.copies(l, c, ph)
        p, _, _ = self.dim(c, ph)
        P, H = self.src(l, c, ph), UNITS[ph] // 2
        rx, tx = self.rx[ph][l * 3 + c], self.tx[ph][l * 3 + c]
        for k, q, off in ((0, (p + 1) % 4, 0), (2, (p + 3) % 4, H)):
            cp(k).wait_recv()
            def add(u, n):
                tx[k // 2, pl.ds(u, n)] = (P[q, pl.ds(off + u, n)].astype(jnp.float32) + rx[k, pl.ds(u, n)].astype(jnp.float32)).astype(jnp.bfloat16)
            self.each(H, add)
            cp(4 + k // 2).start()

    def finish(self, l, c, ph, store):
        cp = self.copies(l, c, ph)
        p, _, _ = self.dim(c, ph)
        P, H = self.src(l, c, ph), UNITS[ph] // 2
        rx = self.rx[ph][l * 3 + c]
        for a, b, off in ((3, 4, 0), (1, 5, H)):
            cp(a).wait_recv()
            cp(b).wait_recv()
            def add(u, n):
                store(off + u, n, P[p, pl.ds(off + u, n)].astype(jnp.float32) + rx[a, pl.ds(u, n)].astype(jnp.float32) + rx[b, pl.ds(u, n)].astype(jnp.float32))
            self.each(H, add)

    @staticmethod
    def each(count, f):
        n = min(count, 4)
        if count == n:
            f(0, n)
        else:
            def body(i, c):
                f(pl.multiple_of(i * n, n), n)
                return c
            lax.fori_loop(0, count // n, body, 0)

    def next_phase(self, l, c, ph):
        t = (self.t1, self.t2)[ph][l * 3 + c]
        per = UNITS[ph + 1]
        def store(u, n, v):
            m = min(n, per)
            for j in range(0, n, m):
                q, r = (u + j) // per, (u + j) % per
                t[q, pl.ds(r, m)] = v[j:j + m].astype(jnp.bfloat16)
        self.finish(l, c, ph, store)
        self.start_a(l, c, ph + 1)

    def last(self, l, c, out):
        w0, w = STARTS[l][c], WIDTHS[l][c]
        def store(u, n, v):
            for j in range(n):
                out[l, (u + j) * 16:(u + j + 1) * 16, w0:w0 + w] = v[j]
        self.finish(l, c, 2, store)

    def put_partial(self, l, x, z, y, val):
        xyz = (x, z, y)
        v = val.astype(jnp.bfloat16).reshape(2, 16, 1024)
        for c in range(3):
            a, b, d = (blend(self.core, xyz[(c + k) % 3], xyz[(c + k + 1) % 3]) for k in range(3))
            w0, w = STARTS[l][c], WIDTHS[l][c]
            self.g[l * 3 + c][a, pl.ds((b * 4 + d) * 2, 2)] = v[:, :, w0:w0 + w]

    def wait_sends(self):
        for l in range(2):
            for c in range(3):
                for ph in range(3):
                    for k in range(6):
                        self.copies(l, c, ph)(k).wait_send()

def scratch():
    lc = [(l, c) for l in range(2) for c in range(3)]
    bf = jnp.bfloat16
    return [
        [pltpu.VMEM((4, 32, 16, WIDTHS[l][c]), bf) for l, c in lc],
        [pltpu.VMEM((4, 8, 16, WIDTHS[l][c]), bf) for l, c in lc],
        [pltpu.VMEM((4, 2, 16, WIDTHS[l][c]), bf) for l, c in lc],
        [[pltpu.VMEM((6, n // 2, 16, WIDTHS[l][c]), bf) for l, c in lc] for n in UNITS],
        [[pltpu.VMEM((2, n // 2, 16, WIDTHS[l][c]), bf) for l, c in lc] for n in UNITS],
        pltpu.SemaphoreType.DMA((6, 3, 6)),
        pltpu.SemaphoreType.DMA((6, 3, 6)),
    ]

def flat(tree):
    return jax.tree.flatten(tree, is_leaf=lambda v: not isinstance(v, list))

def partials(ring, l, nt_ref, delta_ref):
    def group(i, carry):
        rows = pl.ds(pl.multiple_of(i * 256, 256), 256)
        prod = jnp.dot(nt_ref[l, rows, :], delta_ref[l], preferred_element_type=jnp.float32)
        for k in range(8):
            ring.put_partial(l, i // 2, (i % 2) * 2 + k // 4, k % 4, prod[k * 32 : k * 32 + 32])
        return carry

    lax.fori_loop(0, 8, group, 0)


class Scatter:
    def __init__(self, ring, heads, bufs):
        self.ring, self.core, self.heads = ring, ring.core, heads
        self.r, self.f, self.ssem, self.rsem, self.lsem = bufs

    def piece(self, n, ph, q, j, m):
        h, c = n // 3, n % 3
        if ph == 0:
            w0, w = STARTS[h][c], WIDTHS[h][c]
            at = [slice(None)] * 3
            at[(c + m) % 3] = q
            at[(c + m + 1) % 3] = j
            return self.heads.at[(*at, h, slice(None), pl.ds(w0, w))]
        if ph == 1:
            return self.r[0][n].at[q, :, j]
        return self.r[1][n].at[q, j]

    def place(self, n, ph, j, s):
        return self.r[2][n].at[s, j] if ph == 2 else self.r[ph][n].at[j, s]

    def whole(self, n, ph, k):
        return self.r[ph][n].at[0] if k in (1, 3) else self.f[ph][n].at[0]

    def remote(self, n, ph, k, src, dst, to):
        return pltpu.make_async_remote_copy(
            src_ref=src,
            dst_ref=dst,
            send_sem=self.ssem.at[n, ph, k],
            recv_sem=self.rsem.at[n, ph, k],
            device_id=(to, self.core),
            device_id_type=MESH,
        )

    def on_core(self, ph, f):
        if ph:
            f(0)
        else:
            for m in range(2):
                pl.when(self.core == m)(functools.partial(f, m))

    def start(self, h, ph):
        def go(m):
            for c in range(3):
                n = h * 3 + c
                p, right, left = self.ring.dim(c, ph)
                f = self.f[ph][n]
                opposite = (p + 2) % 4
                for i in range(2):
                    self.remote(n, ph, 0, self.piece(n, ph, opposite, i, m), f.at[0, i], right).start()
                    self.remote(n, ph, 2, self.piece(n, ph, opposite, 2 + i, m), f.at[1, i], left).start()
                for j in range(4):
                    self.remote(
                        n, ph, 1, self.piece(n, ph, (p + 1) % 4, j, m), self.place(n, ph, j, p), right
                    ).start()
                    self.remote(
                        n, ph, 3, self.piece(n, ph, (p + 3) % 4, j, m), self.place(n, ph, j, p), left
                    ).start()
                for j in range(4):
                    pltpu.make_async_copy(
                        self.piece(n, ph, p, j, m), self.place(n, ph, j, p), self.lsem.at[n, ph]
                    ).start()

        self.on_core(ph, go)

    def wait(self, n, ph, k, sem):
        ref = self.whole(n, ph, k)
        pltpu.make_async_copy(ref, ref, sem).wait()

    def relay(self, h, ph):
        for c in range(3):
            n = h * 3 + c
            p, right, left = self.ring.dim(c, ph)
            f = self.f[ph][n]
            self.wait(n, ph, 0, self.rsem.at[n, ph, 0])
            for i in range(2):
                self.remote(n, ph, 4, f.at[0, i], self.place(n, ph, i, (p + 3) % 4), right).start()
            self.wait(n, ph, 2, self.rsem.at[n, ph, 2])
            for i in range(2):
                self.remote(n, ph, 5, f.at[1, i], self.place(n, ph, 2 + i, (p + 1) % 4), left).start()

    def finish(self, h, ph):
        for c in range(3):
            n = h * 3 + c
            self.wait(n, ph, 1, self.lsem.at[n, ph])
            for k in (1, 3, 4, 5):
                self.wait(n, ph, k, self.rsem.at[n, ph, k])

    def wait_sends(self):
        for n in range(6):
            for ph in range(3):
                for k in range(6):
                    self.wait(n, ph, k, self.ssem.at[n, ph, k])

    def owners_of(self, c):
        return tuple(
            blend(self.core, STRIDES[(c + k) % 3], STRIDES[(c + k + 1) % 3]) for k in range(3)
        )


def scatter_scratch():
    hc = [(h, c) for h in range(2) for c in range(3)]
    bf = jnp.bfloat16
    return [
        [[pltpu.VMEM((4, 4, 4, 16, WIDTHS[h][c]), bf) for h, c in hc] for _ in range(3)],
        [[pltpu.VMEM((2, 2, 4, 16, WIDTHS[h][c]), bf) for h, c in hc] for _ in range(3)],
        pltpu.SemaphoreType.DMA((6, 3, 6)),
        pltpu.SemaphoreType.DMA((6, 3, 6)),
        pltpu.SemaphoreType.DMA((6, 3)),
    ]


LIVE = 256
HALF = 1024
FULL = 2048
C0 = math.sqrt(2 / math.pi)
C1 = 0.044715


def work_scratch():
    f32, bf = jnp.float32, jnp.bfloat16
    return [
        pltpu.VMEM((2, FULL, HALF), bf),
        [pltpu.VMEM((2, LIVE, HALF), bf) for _ in range(2)],
        pltpu.VMEM((LIVE, HALF), bf),
        pltpu.VMEM((LIVE, FULL), bf),
        pltpu.VMEM((2, FULL, LIVE), bf),
        pltpu.VMEM((LIVE, 128), f32),
        pltpu.VMEM((2, LIVE, HALF), f32),
        pltpu.VMEM((LIVE, HALF), f32),
        pltpu.VMEM((LIVE, HALF), f32),
        pltpu.VMEM((2, LIVE, HALF), bf),
        pltpu.VMEM((2, 32, LIVE), f32),
        pltpu.VMEM((LIVE, 128), f32),
        pltpu.VMEM((LIVE, HALF), bf),
        pltpu.VMEM((2, LIVE, 128), f32),
        pltpu.VMEM((2, 4, LIVE, 256), bf),
        pltpu.VMEM((4, LIVE, 256), f32),
        pltpu.SemaphoreType.DMA((4,)),
        pltpu.SemaphoreType.DMA((8,)),
        pltpu.SemaphoreType.DMA((8,)),
    ]


def loop(count, f):
    def go(i, carry):
        f(i)
        return carry

    lax.fori_loop(0, count, go, 0)


def mega_kernel(tree, feats, gains, weights, heads, lengths, owners, labels, grads, loss, *refs):
    me, core = lax.axis_index("dp"), lax.axis_index("mp")
    ring_bufs, scatter_bufs, work = jax.tree.unflatten(tree, refs)
    (wts, xs, x2, nrm, nrm_t, r1, dgelu, pre1, up, delta, logit, owner_down, spread, stat, dn, dn_own, lsem, ssem, rsem) = work
    ring = Ring(me, core, ring_bufs)
    scatter = Scatter(ring, heads, scatter_bufs)
    other = 1 - core
    f32, bf = jnp.float32, jnp.bfloat16

    load = [pltpu.make_async_copy(weights.at[l], wts.at[l], lsem.at[l]) for l in range(2)]
    own_x = pltpu.make_async_copy(feats.at[pl.ds(0, LIVE)], xs[0].at[core], lsem.at[2])
    own_x.start()
    for cp in load:
        cp.start()

    def swap(k, src, dst):
        return pltpu.make_async_remote_copy(
            src_ref=src,
            dst_ref=dst,
            send_sem=ssem.at[k],
            recv_sem=rsem.at[k],
            device_id=(me, other),
            device_id_type=MESH,
        )

    bar = pltpu.get_barrier_semaphore()
    pl.semaphore_signal(bar, inc=1, device_id=(me, other), device_id_type=MESH)
    for s in STRIDES:
        p = (me // s) % 4
        for step in (1, 3):
            to = me + ((p + step) % 4 - p) * s
            pl.semaphore_signal(bar, inc=1, device_id=(to, core), device_id_type=MESH)
    pl.semaphore_wait(bar, 7)

    swap_x = [swap(0, feats.at[pl.ds(0, LIVE)], xs[0].at[core]), swap(1, xs[1].at[core], xs[1].at[core])]
    swap_x[0].start()
    for h in range(2):
        scatter.start(h, 0)

    def down(row):
        same = lax.broadcasted_iota(jnp.int32, (64, 64), 0) == lax.broadcasted_iota(jnp.int32, (64, 64), 1)
        return jnp.sum(jnp.where(same, row, 0), 1, keepdims=True)

    lens = lengths[...]
    upto = lax.broadcasted_iota(jnp.int32, (64, 64), 1) <= lax.broadcasted_iota(jnp.int32, (64, 64), 0)
    ends = jnp.sum(jnp.where(upto, lens, 0), 1, keepdims=True)
    lens_down = down(lens)
    slot = lax.broadcasted_iota(jnp.int32, (64, LIVE), 1)
    here = (slot < ends) & (slot >= ends - lens_down)
    slot_owner = jnp.sum(jnp.where(here, down(owners[...]), 0), 0, keepdims=True)
    slot_len = jnp.sum(jnp.where(here, lens_down, 0), 0, keepdims=True)
    owner_down[...] = jnp.broadcast_to(slot_owner.astype(f32), (128, LIVE)).T

    def layer(l):
        def norm(i):
            rows = pl.ds(pl.multiple_of(i * 32, 32), 32)
            a, b = xs[l][0, rows, :].astype(f32), xs[l][1, rows, :].astype(f32)
            mean = (jnp.sum(a * a, -1, keepdims=True) + jnp.sum(b * b, -1, keepdims=True)) * (1.0 / FULL)
            scale = lax.rsqrt(mean + EPSILON)
            nrm[rows, 0:HALF] = (a * scale * gains[l : l + 1, 0:HALF]).astype(bf)
            nrm[rows, HALF:FULL] = (b * scale * gains[l : l + 1, HALF:FULL]).astype(bf)
            if l == 1:
                r1[rows, :] = jnp.broadcast_to(scale, (32, 128))

        loop(LIVE // 32, norm)

        def columns(i):
            cols = pl.ds(pl.multiple_of(i * 256, 256), 256)
            pre = jnp.dot(nrm[...], wts[l, :, cols], preferred_element_type=f32)
            t = jnp.tanh(C0 * (pre + C1 * (pre * pre * pre)))
            half = 0.5 * (1.0 + t)
            dgelu[l, :, cols] = half + 0.5 * pre * (1.0 - t * t) * (C0 * (1.0 + 3.0 * C1 * (pre * pre)))
            out = (xs[l][core, :, cols].astype(f32) + pre * half).astype(bf)
            if l == 0:
                xs[1][core, :, cols] = out
            else:
                x2[:, cols] = out
                pre1[:, cols] = pre

        loop(HALF // 256, columns)
        if l == 0:
            swap_x[1].start()

        def turn(i):
            cols = pl.ds(pl.multiple_of(i * 256, 256), 256)
            nrm_t[l, cols, :] = nrm[:, cols].astype(f32).T.astype(bf)

        loop(FULL // 256, turn)

    own_x.wait()
    swap_x[0].wait_recv()
    load[0].wait()
    layer(0)
    scatter.relay(0, 0)
    swap_x[1].wait_recv()
    load[1].wait()
    layer(1)
    scatter.relay(1, 0)
    for ph in range(2):
        for h in range(2):
            scatter.finish(h, ph)
            scatter.start(h, ph + 1)
        for h in range(2):
            scatter.relay(h, ph + 1)

    for h in range(2):
        scatter.finish(h, 2)
        total = jnp.zeros((16, LIVE), f32)
        for c in range(3):
            w0, w = STARTS[h][c], WIDTHS[h][c]
            sa, sb, sc = scatter.owners_of(c)
            block = scatter.r[2][h * 3 + c]

            def pick(i, acc):
                part = block[i].reshape(256, w)
                prod = lax.dot_general(
                    part, x2[:, w0 : w0 + w], (((1,), (1,)), ((), ())), preferred_element_type=f32
                )
                for k in range(16):
                    owner = (k % 4) * sa + (k // 4) * sb + i * sc
                    acc = acc + jnp.where(slot_owner == owner, prod[k * 16 : k * 16 + 16], 0.0)
                return acc

            total = lax.fori_loop(0, 4, pick, total)
        logit[0, 16 * h : 16 * h + 16, :] = total
    swap_logit = swap(2, logit.at[0], logit.at[1])
    swap_logit.start()
    swap_logit.wait_recv()
    scores = logit[0] + logit[1]
    hit = lax.broadcasted_iota(jnp.int32, (32, LIVE), 0) == labels[0:1, 0:LIVE]
    log_total = jnp.log(jnp.sum(jnp.exp(scores), 0, keepdims=True))
    picked = jnp.sum(jnp.where(hit, scores, 0.0), 0, keepdims=True)
    loss[0:1, 0:LIVE] = (log_total - picked).astype(bf)
    loss[0:1, LIVE : 2 * LIVE] = jnp.zeros((1, LIVE), bf)
    dlogits = (jnp.exp(scores - log_total) - hit.astype(f32)) * (1.0 / slot_len.astype(f32))

    group = lax.broadcasted_iota(jnp.int32, (1, 128), 1) // 16
    for h in range(2):
        tiled = jnp.concatenate([dlogits[16 * h : 16 * h + 16]] * 8, axis=0).T
        for c in range(3):
            w0, w = STARTS[h][c], WIDTHS[h][c]
            sa, sb, sc = scatter.owners_of(c)
            for j in range(8):
                owner = (group % 4) * sa + (2 * (j % 2) + group // 4) * sb + (j // 2) * sc
                spread[:, 128 * j : 128 * j + 128] = jnp.where(
                    owner_down[...] == owner.astype(f32), tiled, 0.0
                ).astype(bf)
            block = scatter.r[2][h * 3 + c]
            grad = jnp.dot(spread[...], block[...].reshape(1024, w), preferred_element_type=f32)
            cols = slice(w0, w0 + w)
            up[:, cols] = grad if h == 0 else up[:, cols] + grad

    def back(i):
        rows = pl.ds(pl.multiple_of(i * 32, 32), 32)
        u = up[rows, :].astype(bf).astype(f32)
        up[rows, :] = u
        d = (u * dgelu[1, rows, :]).astype(bf)
        delta[1, rows, :] = d
        row = jnp.sum(d.astype(f32) * pre1[rows, :], -1, keepdims=True)
        stat[0, rows, :] = jnp.broadcast_to(row, (32, 128)) / r1[rows, :]

    loop(LIVE // 32, back)
    swap_stat = swap(3, stat.at[0], stat.at[1])
    swap_stat.start()

    def begin(l):
        partials(ring, l, nrm_t, delta)
        for c in range(3):
            ring.start_a(l, c, 0)

    begin(1)
    swap_dn = [swap(4 + i, dn.at[0, i], dn.at[1, i]) for i in range(4)]
    for i in range(4):
        part = wts[1, pl.ds(pl.multiple_of(other * HALF + i * 256, 256), 256), :]
        dn[0, i] = lax.dot_general(
            delta[1], part, (((1,), (1,)), ((), ())), preferred_element_type=f32
        ).astype(bf)
        swap_dn[i].start()

    def own_part(i):
        part = wts[1, pl.ds(pl.multiple_of(core * HALF + i * 256, 256), 256), :]
        dn_own[i] = lax.dot_general(delta[1], part, (((1,), (1,)), ((), ())), preferred_element_type=f32)

    loop(4, own_part)
    swap_stat.wait_recv()
    for i in range(4):
        swap_dn[i].wait_recv()
        cols = slice(256 * i, 256 * i + 256)
        gain = jnp.where(core == 0, gains[1:2, 256 * i : 256 * i + 256], gains[1:2, HALF + 256 * i : HALF + 256 * i + 256])

        def dx(k):
            rows = pl.ds(pl.multiple_of(k * 64, 64), 64)
            scale = r1[rows, 0:1]
            cross = (stat[0, rows, 0:1] + stat[1, rows, 0:1]) * (1.0 / FULL)
            d = (
                up[rows, cols]
                + gain * scale * (dn_own[i, rows, :] + dn[1, i, rows, :].astype(f32))
                - xs[1][core, rows, cols].astype(f32) * (scale * scale * scale * cross)
            )
            delta[0, rows, cols] = (d * dgelu[0, rows, cols]).astype(bf)

        loop(LIVE // 64, dx)
    begin(0)
    for ph in range(3):
        for l in (1, 0):
            for c in range(3):
                ring.step_b(l, c, ph)
        for l in (1, 0):
            for c in range(3):
                if ph < 2:
                    ring.next_phase(l, c, ph)
                else:
                    ring.last(l, c, grads)
    ring.wait_sends()
    scatter.wait_sends()
    for cp in (*swap_x, swap_logit, swap_stat, *swap_dn):
        cp.wait_send()


def body(features, gains, weights, heads, lengths, owners, labels):
    slots = features.shape[0]
    leaves, tree = flat([scratch(), scatter_scratch(), work_scratch()])
    vmem, hbm = pl.BlockSpec(memory_space=pltpu.VMEM), pl.BlockSpec(memory_space=pl.ANY)
    grads, loss = pl.pallas_call(
        functools.partial(mega_kernel, tree),
        out_shape=(
            jax.ShapeDtypeStruct((2, 32, HALF), jnp.float32),
            jax.ShapeDtypeStruct((1, slots), jnp.bfloat16),
        ),
        in_specs=[hbm, vmem, hbm, hbm, vmem, vmem, vmem],
        out_specs=(vmem, vmem),
        scratch_shapes=leaves,
        compiler_params=pltpu.CompilerParams(
            collective_id=0, has_side_effects=True, vmem_limit_bytes=67043328
        ),
        name="step",
    )(
        features,
        gains,
        weights,
        heads.reshape(4, 4, 4, 2, 16, HALF),
        lengths,
        owners,
        labels.reshape(1, slots),
    )
    return (grads, loss.reshape(slots))


def solution(mesh):
    return jax.shard_map(
        body,
        mesh=mesh,
        in_specs=(
            P("dp", "mp"),
            P(),
            P(None, None, "mp"),
            P("dp", None, "mp"),
            P("dp", None),
            P("dp", None),
            P("dp"),
        ),
        out_specs=(P(None, "dp", "mp"), P("dp")),
        check_vma=False,
    )
```

```python
import functools
import math

import jax
import jax.numpy as jnp
from jax import lax
from jax.experimental import pallas as pl
from jax.experimental.pallas import tpu as pltpu
from jax.sharding import PartitionSpec as P

EPSILON = 1e-06
MESH = pl.DeviceIdType.MESH
STRIDES = (16, 4, 1)
WIDTHS = ((384, 256, 384), (384, 384, 256))
STARTS = tuple(tuple(sum(w[:k]) for k in range(3)) for w in WIDTHS)
UNITS = (16, 4, 1)

def blend(core, a, b):
    return a + core * (b - a)

class Ring:
    def __init__(self, me, core, bufs):
        self.me, self.core = me, core
        self.g, self.t1, self.t2, self.rx, self.tx, self.ssem, self.rsem = bufs
        self.coords = tuple((me // s) % 4 for s in STRIDES)

    def dim(self, c, ph):
        k0, k1 = (c + ph) % 3, (c + ph + 1) % 3
        stride = blend(self.core, STRIDES[k0], STRIDES[k1])
        p = blend(self.core, self.coords[k0], self.coords[k1])
        right = self.me + ((p + 1) % 4 - p) * stride
        left = self.me + ((p + 3) % 4 - p) * stride
        return p, right, left

    def copies(self, k, c, ph):
        p, right, left = self.dim(c, ph)
        n = k * 3 + c
        part = (self.g, self.t1, self.t2)[ph][n]
        half = UNITS[ph] // 2
        lo, hi = pl.ds(0, half), pl.ds(half, half)

        def nth(i):
            if ph == 2:
                src = part.at[(p + (1, 3, 2)[i]) % 4]
                stride = blend(self.core, STRIDES[(c + 2) % 3], STRIDES[c])
                to = (right, left, self.me + ((p + 2) % 4 - p) * stride)[i]
            elif i < 4:
                src = part.at[(p + (2, 1, 2, 3)[i]) % 4, (lo, hi, hi, lo)[i]]
                to = (right, right, left, left)[i]
            else:
                src = self.tx[ph][n].at[i - 4]
                to = (right, left)[i - 4]
            return pltpu.make_async_remote_copy(
                src_ref=src,
                dst_ref=self.rx[ph][n].at[i],
                send_sem=self.ssem.at[n, ph, i],
                recv_sem=self.rsem.at[n, ph, i],
                device_id=(to, self.core),
                device_id_type=MESH,
            )

        return nth

    def start(self, k, c, ph):
        cp = self.copies(k, c, ph)
        for i in (0, 1, 2) if ph == 2 else (0, 2, 1, 3):
            cp(i).start()

    def forward(self, k, ph):
        half = UNITS[ph] // 2
        for c in range(3):
            n = k * 3 + c
            cp = self.copies(k, c, ph)
            p, _, _ = self.dim(c, ph)
            part, rx, tx = (self.g, self.t1)[ph][n], self.rx[ph][n], self.tx[ph][n]
            for i, q, off in ((0, (p + 1) % 4, 0), (2, (p + 3) % 4, half)):
                cp(i).wait_recv()

                def add(u, m):
                    tx[i // 2, pl.ds(u, m)] = (
                        part[q, pl.ds(off + u, m)].astype(jnp.float32)
                        + rx[i, pl.ds(u, m)].astype(jnp.float32)
                    ).astype(jnp.bfloat16)

                self.each(half, add)
                cp(4 + i // 2).start()

    def finish(self, k, ph):
        half, per = UNITS[ph] // 2, UNITS[ph + 1]
        for c in range(3):
            n = k * 3 + c
            cp = self.copies(k, c, ph)
            p, _, _ = self.dim(c, ph)
            part, rx, t = (self.g, self.t1)[ph][n], self.rx[ph][n], (self.t1, self.t2)[ph][n]
            for a, b, off in ((3, 4, 0), (1, 5, half)):
                cp(a).wait_recv()
                cp(b).wait_recv()

                def add(u, m):
                    v = (
                        part[p, pl.ds(off + u, m)].astype(jnp.float32)
                        + rx[a, pl.ds(u, m)].astype(jnp.float32)
                        + rx[b, pl.ds(u, m)].astype(jnp.float32)
                    ).astype(jnp.bfloat16)
                    for q in range(m // per):
                        t[(off + u) // per + q] = v[q * per : (q + 1) * per]

                self.each(half, add)
            self.start(k, c, ph + 1)

    def last(self, k, out):
        l, r = k // 2, k % 2
        for c in range(3):
            n = k * 3 + c
            cp = self.copies(k, c, 2)
            p, _, _ = self.dim(c, 2)
            for i in range(3):
                cp(i).wait_recv()
            total = self.t2[n][p, 0].astype(jnp.float32)
            for i in range(3):
                total = total + self.rx[2][n][i, 0].astype(jnp.float32)
            w0, w = STARTS[l][c], WIDTHS[l][c]
            out[l, 16 * r : 16 * r + 16, w0 : w0 + w] = total

    @staticmethod
    def each(count, f):
        n = min(count, 4)
        if count == n:
            f(0, n)
        else:

            def go(i, carry):
                f(pl.multiple_of(i * n, n), n)
                return carry

            lax.fori_loop(0, count // n, go, 0)

    def wait_sends(self):
        for k in range(4):
            for c in range(3):
                for ph in range(3):
                    for i in range(3 if ph == 2 else 6):
                        self.copies(k, c, ph)(i).wait_send()


def ring_scratch():
    bf = jnp.bfloat16
    widths = [WIDTHS[k // 2][c] for k in range(4) for c in range(3)]
    return [
        *[[pltpu.VMEM((4, n, 16, w), bf) for w in widths] for n in UNITS],
        [[pltpu.VMEM((6, n // 2, 16, w) if n > 1 else (3, 1, 16, w), bf) for w in widths] for n in UNITS],
        [[pltpu.VMEM((2, n // 2, 16, w), bf) for w in widths] for n in UNITS[:2]],
        pltpu.SemaphoreType.DMA((12, 3, 6)),
        pltpu.SemaphoreType.DMA((12, 3, 6)),
    ]


def flat(tree):
    return jax.tree.flatten(tree, is_leaf=lambda v: not isinstance(v, list))


def begin(ring, k, nt_ref, delta_ref):
    l, r = k // 2, k % 2
    for c in range(3):
        w0, w = STARTS[l][c], WIDTHS[l][c]
        g = ring.g[k * 3 + c]

        def group(x, carry):
            rows = pl.ds(pl.multiple_of(x * 256, 256), 256)
            prod = jnp.dot(
                nt_ref[l, r, rows, :], delta_ref[l, :, w0 : w0 + w], preferred_element_type=jnp.float32
            )
            v = prod.astype(jnp.bfloat16).reshape(16, 16, w)
            for i in range(16):
                xyz = (x, i // 4, i % 4)
                a, b, d = (
                    blend(ring.core, xyz[(c + e) % 3], xyz[(c + e + 1) % 3]) for e in range(3)
                )
                g[a, b * 4 + d] = v[i]
            return carry

        lax.fori_loop(0, 4, group, 0)
        ring.start(k, c, 0)


class Scatter:
    def __init__(self, ring, heads, bufs):
        self.ring, self.core, self.heads = ring, ring.core, heads
        self.r, self.f, self.ssem, self.rsem, self.lsem = bufs

    def piece(self, n, ph, q, j, m):
        h, c = n // 3, n % 3
        if ph == 0:
            w0, w = STARTS[h][c], WIDTHS[h][c]
            at = [slice(None)] * 3
            at[(c + m) % 3] = q
            at[(c + m + 1) % 3] = j
            return self.heads.at[(*at, h, slice(None), pl.ds(w0, w))]
        if ph == 1:
            return self.r[0][n].at[q, :, j]
        return self.r[1][n].at[q, j]

    def place(self, n, ph, j, s):
        return self.r[2][n].at[s, j] if ph == 2 else self.r[ph][n].at[j, s]

    def whole(self, n, ph, k):
        return self.r[ph][n].at[0] if k in (1, 3) else self.f[ph][n].at[0]

    def remote(self, n, ph, k, src, dst, to):
        return pltpu.make_async_remote_copy(
            src_ref=src,
            dst_ref=dst,
            send_sem=self.ssem.at[n, ph, k],
            recv_sem=self.rsem.at[n, ph, k],
            device_id=(to, self.core),
            device_id_type=MESH,
        )

    def on_core(self, ph, f):
        if ph:
            f(0)
        else:
            for m in range(2):
                pl.when(self.core == m)(functools.partial(f, m))

    def start(self, h, ph):
        def go(m):
            for c in range(3):
                n = h * 3 + c
                p, right, left = self.ring.dim(c, ph)
                f = self.f[ph][n]
                opposite = (p + 2) % 4
                for i in range(2):
                    self.remote(n, ph, 0, self.piece(n, ph, opposite, i, m), f.at[0, i], right).start()
                    self.remote(n, ph, 2, self.piece(n, ph, opposite, 2 + i, m), f.at[1, i], left).start()
                for j in range(4):
                    self.remote(
                        n, ph, 1, self.piece(n, ph, (p + 1) % 4, j, m), self.place(n, ph, j, p), right
                    ).start()
                    self.remote(
                        n, ph, 3, self.piece(n, ph, (p + 3) % 4, j, m), self.place(n, ph, j, p), left
                    ).start()
                for j in range(4):
                    pltpu.make_async_copy(
                        self.piece(n, ph, p, j, m), self.place(n, ph, j, p), self.lsem.at[n, ph]
                    ).start()

        self.on_core(ph, go)

    def wait(self, n, ph, k, sem):
        ref = self.whole(n, ph, k)
        pltpu.make_async_copy(ref, ref, sem).wait()

    def relay(self, h, ph):
        for c in range(3):
            n = h * 3 + c
            p, right, left = self.ring.dim(c, ph)
            f = self.f[ph][n]
            self.wait(n, ph, 0, self.rsem.at[n, ph, 0])
            for i in range(2):
                self.remote(n, ph, 4, f.at[0, i], self.place(n, ph, i, (p + 3) % 4), right).start()
            self.wait(n, ph, 2, self.rsem.at[n, ph, 2])
            for i in range(2):
                self.remote(n, ph, 5, f.at[1, i], self.place(n, ph, 2 + i, (p + 1) % 4), left).start()

    def finish(self, h, ph):
        for c in range(3):
            n = h * 3 + c
            self.wait(n, ph, 1, self.lsem.at[n, ph])
            for k in (1, 3, 4, 5):
                self.wait(n, ph, k, self.rsem.at[n, ph, k])

    def wait_sends(self):
        for n in range(6):
            for ph in range(3):
                for k in range(6):
                    self.wait(n, ph, k, self.ssem.at[n, ph, k])

    def owners_of(self, c):
        return tuple(
            blend(self.core, STRIDES[(c + k) % 3], STRIDES[(c + k + 1) % 3]) for k in range(3)
        )


def scatter_scratch():
    hc = [(h, c) for h in range(2) for c in range(3)]
    bf = jnp.bfloat16
    return [
        [[pltpu.VMEM((4, 4, 4, 16, WIDTHS[h][c]), bf) for h, c in hc] for _ in range(3)],
        [[pltpu.VMEM((2, 2, 4, 16, WIDTHS[h][c]), bf) for h, c in hc] for _ in range(3)],
        pltpu.SemaphoreType.DMA((6, 3, 6)),
        pltpu.SemaphoreType.DMA((6, 3, 6)),
        pltpu.SemaphoreType.DMA((6, 3)),
    ]


LIVE = 256
HALF = 1024
FULL = 2048
C0 = math.sqrt(2 / math.pi)
C1 = 0.044715


def work_scratch():
    f32, bf = jnp.float32, jnp.bfloat16
    return [
        pltpu.VMEM((2, FULL, HALF), bf),
        [pltpu.VMEM((2, LIVE, HALF), bf) for _ in range(2)],
        pltpu.VMEM((LIVE, HALF), bf),
        pltpu.VMEM((LIVE, FULL), bf),
        pltpu.VMEM((2, 2, HALF, LIVE), bf),
        pltpu.VMEM((LIVE, 128), f32),
        pltpu.VMEM((2, LIVE, HALF), f32),
        pltpu.VMEM((LIVE, HALF), f32),
        pltpu.VMEM((LIVE, HALF), f32),
        pltpu.VMEM((2, LIVE, HALF), bf),
        pltpu.VMEM((2, 32, LIVE), f32),
        pltpu.VMEM((LIVE, 128), f32),
        pltpu.VMEM((LIVE, HALF), bf),
        pltpu.VMEM((2, LIVE, 128), f32),
        pltpu.VMEM((2, 4, LIVE, 256), bf),
        pltpu.VMEM((4, LIVE, 256), f32),
        pltpu.VMEM((2, FULL), f32),
        pltpu.VMEM((1, 64), jnp.int32),
        pltpu.VMEM((1, 64), jnp.int32),
        pltpu.VMEM((1, 2 * LIVE), jnp.int32),
        pltpu.SemaphoreType.DMA((8,)),
        pltpu.SemaphoreType.DMA((8,)),
        pltpu.SemaphoreType.DMA((8,)),
    ]


def loop(count, f):
    def go(i, carry):
        f(i)
        return carry

    lax.fori_loop(0, count, go, 0)


def mega_kernel(tree, feats, gains_hbm, weights, heads, lengths_hbm, owners_hbm, labels_hbm, grads, loss, *refs):
    me, core = lax.axis_index("dp"), lax.axis_index("mp")
    ring_bufs, scatter_bufs, work = jax.tree.unflatten(tree, refs)
    (wts, xs, x2, nrm, nrm_t, r1, dgelu, pre1, up, delta, logit, owner_down, spread, stat, dn, dn_own, gains, lengths, owners, labels, lsem, ssem, rsem) = work
    ring = Ring(me, core, ring_bufs)
    scatter = Scatter(ring, heads, scatter_bufs)
    other = 1 - core
    f32, bf = jnp.float32, jnp.bfloat16

    load = [pltpu.make_async_copy(weights.at[l], wts.at[l], lsem.at[l]) for l in range(2)]
    own_x = pltpu.make_async_copy(feats.at[pl.ds(0, LIVE)], xs[0].at[core], lsem.at[2])
    small = [
        pltpu.make_async_copy(src, dst, lsem.at[3 + i])
        for i, (src, dst) in enumerate(
            ((gains_hbm, gains), (lengths_hbm, lengths), (owners_hbm, owners), (labels_hbm, labels))
        )
    ]
    for cp in (own_x, *small, *load):
        cp.start()

    def swap(k, src, dst):
        return pltpu.make_async_remote_copy(
            src_ref=src,
            dst_ref=dst,
            send_sem=ssem.at[k],
            recv_sem=rsem.at[k],
            device_id=(me, other),
            device_id_type=MESH,
        )

    bar = pltpu.get_barrier_semaphore()
    pl.semaphore_signal(bar, inc=1, device_id=(me, other), device_id_type=MESH)
    for s in STRIDES:
        p = (me // s) % 4
        for step in (1, 3):
            to = me + ((p + step) % 4 - p) * s
            pl.semaphore_signal(bar, inc=1, device_id=(to, core), device_id_type=MESH)
    pl.semaphore_wait(bar, 7)

    swap_x = [swap(0, feats.at[pl.ds(0, LIVE)], xs[0].at[core]), swap(1, xs[1].at[core], xs[1].at[core])]
    swap_x[0].start()
    for h in range(2):
        scatter.start(h, 0)

    def down(row):
        same = lax.broadcasted_iota(jnp.int32, (64, 64), 0) == lax.broadcasted_iota(jnp.int32, (64, 64), 1)
        return jnp.sum(jnp.where(same, row, 0), 1, keepdims=True)

    for cp in small:
        cp.wait()
    lens = lengths[...]
    upto = lax.broadcasted_iota(jnp.int32, (64, 64), 1) <= lax.broadcasted_iota(jnp.int32, (64, 64), 0)
    ends = jnp.sum(jnp.where(upto, lens, 0), 1, keepdims=True)
    lens_down = down(lens)
    slot = lax.broadcasted_iota(jnp.int32, (64, LIVE), 1)
    here = (slot < ends) & (slot >= ends - lens_down)
    slot_owner = jnp.sum(jnp.where(here, down(owners[...]), 0), 0, keepdims=True)
    slot_len = jnp.sum(jnp.where(here, lens_down, 0), 0, keepdims=True)
    owner_down[...] = jnp.broadcast_to(slot_owner.astype(f32), (128, LIVE)).T

    def norm_layer(l):
        def norm(i):
            rows = pl.ds(pl.multiple_of(i * 32, 32), 32)
            a, b = xs[l][0, rows, :].astype(f32), xs[l][1, rows, :].astype(f32)
            mean = (jnp.sum(a * a, -1, keepdims=True) + jnp.sum(b * b, -1, keepdims=True)) * (1.0 / FULL)
            scale = lax.rsqrt(mean + EPSILON)
            nrm[rows, 0:HALF] = (a * scale * gains[l : l + 1, 0:HALF]).astype(bf)
            nrm[rows, HALF:FULL] = (b * scale * gains[l : l + 1, HALF:FULL]).astype(bf)
            if l == 1:
                r1[rows, :] = jnp.broadcast_to(scale, (32, 128))

        loop(LIVE // 32, norm)

    def main_layer(l):
        def columns(i):
            cols = pl.ds(pl.multiple_of(i * 256, 256), 256)
            pre = jnp.dot(nrm[...], wts[l, :, cols], preferred_element_type=f32)
            t = jnp.tanh(C0 * (pre + C1 * (pre * pre * pre)))
            half = 0.5 * (1.0 + t)
            dgelu[l, :, cols] = half + 0.5 * pre * (1.0 - t * t) * (C0 * (1.0 + 3.0 * C1 * (pre * pre)))
            out = (xs[l][core, :, cols].astype(f32) + pre * half).astype(bf)
            if l == 0:
                xs[1][core, :, cols] = out
            else:
                x2[:, cols] = out
                pre1[:, cols] = pre

        loop(HALF // 256, columns)
        if l == 0:
            swap_x[1].start()

    def turn_layer(l):
        def turn(i):
            cols = pl.ds(pl.multiple_of(i * 256, 256), 256)
            turned = nrm[:, cols].astype(f32).T.astype(bf).reshape(8, 2, 16, LIVE)
            for k in range(2):
                nrm_t[l, k, pl.ds(pl.multiple_of(i * 128, 128), 128), :] = turned[:, k].reshape(128, LIVE)

        loop(FULL // 256, turn)

    own_x.wait()
    swap_x[0].wait_recv()
    norm_layer(0)
    load[0].wait()
    main_layer(0)
    scatter.relay(0, 0)
    turn_layer(0)
    swap_x[1].wait_recv()
    norm_layer(1)
    scatter.relay(1, 0)
    load[1].wait()
    main_layer(1)
    scatter.finish(0, 0)
    scatter.start(0, 1)
    scatter.finish(1, 0)
    scatter.start(1, 1)
    turn_layer(1)
    for h in range(2):
        scatter.relay(h, 1)
    for h in range(2):
        scatter.finish(h, 1)
        scatter.start(h, 2)
    for h in range(2):
        scatter.relay(h, 2)

    for h in range(2):
        scatter.finish(h, 2)
        total = jnp.zeros((16, LIVE), f32)
        for c in range(3):
            w0, w = STARTS[h][c], WIDTHS[h][c]
            sa, sb, sc = scatter.owners_of(c)
            block = scatter.r[2][h * 3 + c]

            prod = lax.dot_general(
                block[...].reshape(1024, w),
                x2[:, w0 : w0 + w],
                (((1,), (1,)), ((), ())),
                preferred_element_type=f32,
            )
            for k in range(64):
                owner = (k % 4) * sa + (k // 4 % 4) * sb + (k // 16) * sc
                total = total + jnp.where(slot_owner == owner, prod[k * 16 : k * 16 + 16], 0.0)
        logit[0, 16 * h : 16 * h + 16, :] = total
    swap_logit = swap(2, logit.at[0], logit.at[1])
    swap_logit.start()
    swap_logit.wait_recv()
    scores = logit[0] + logit[1]
    hit = lax.broadcasted_iota(jnp.int32, (32, LIVE), 0) == labels[0:1, 0:LIVE]
    log_total = jnp.log(jnp.sum(jnp.exp(scores), 0, keepdims=True))
    picked = jnp.sum(jnp.where(hit, scores, 0.0), 0, keepdims=True)
    losses = (log_total - picked).astype(bf)
    loss[0:1, :] = losses[:, 0:128]
    loss[1:2, :] = losses[:, 128:LIVE]
    loss[2:4, :] = jnp.zeros((2, 128), bf)
    dlogits = (jnp.exp(scores - log_total) - hit.astype(f32)) * (1.0 / slot_len.astype(f32))

    group = lax.broadcasted_iota(jnp.int32, (1, 128), 1) // 16
    for h in range(2):
        tiled = jnp.concatenate([dlogits[16 * h : 16 * h + 16]] * 8, axis=0).T
        for c in range(3):
            w0, w = STARTS[h][c], WIDTHS[h][c]
            sa, sb, sc = scatter.owners_of(c)
            for j in range(8):
                owner = (group % 4) * sa + (2 * (j % 2) + group // 4) * sb + (j // 2) * sc
                spread[:, 128 * j : 128 * j + 128] = jnp.where(
                    owner_down[...] == owner.astype(f32), tiled, 0.0
                ).astype(bf)
            block = scatter.r[2][h * 3 + c]
            grad = jnp.dot(spread[...], block[...].reshape(1024, w), preferred_element_type=f32)
            cols = slice(w0, w0 + w)
            up[:, cols] = grad if h == 0 else up[:, cols] + grad

    def back(i):
        rows = pl.ds(pl.multiple_of(i * 32, 32), 32)
        u = up[rows, :].astype(bf).astype(f32)
        up[rows, :] = u
        d = (u * dgelu[1, rows, :]).astype(bf)
        delta[1, rows, :] = d
        row = jnp.sum(d.astype(f32) * pre1[rows, :], -1, keepdims=True)
        stat[0, rows, :] = jnp.broadcast_to(row, (32, 128)) / r1[rows, :]

    loop(LIVE // 32, back)
    swap_stat = swap(3, stat.at[0], stat.at[1])
    swap_stat.start()

    for k in (2, 3):
        begin(ring, k, nrm_t, delta)
    swap_dn = [swap(4 + i, dn.at[0, i], dn.at[1, i]) for i in range(4)]
    for i in range(4):
        part = wts[1, pl.ds(pl.multiple_of(other * HALF + i * 256, 256), 256), :]
        dn[0, i] = lax.dot_general(
            delta[1], part, (((1,), (1,)), ((), ())), preferred_element_type=f32
        ).astype(bf)
        swap_dn[i].start()
    ring.forward(2, 0)

    def own_part(i):
        part = wts[1, pl.ds(pl.multiple_of(core * HALF + i * 256, 256), 256), :]
        dn_own[i] = lax.dot_general(delta[1], part, (((1,), (1,)), ((), ())), preferred_element_type=f32)

    loop(4, own_part)
    swap_stat.wait_recv()
    for i in range(4):
        swap_dn[i].wait_recv()
        cols = slice(256 * i, 256 * i + 256)
        gain = jnp.where(core == 0, gains[1:2, 256 * i : 256 * i + 256], gains[1:2, HALF + 256 * i : HALF + 256 * i + 256])

        def dx(k):
            rows = pl.ds(pl.multiple_of(k * 64, 64), 64)
            scale = r1[rows, 0:1]
            cross = (stat[0, rows, 0:1] + stat[1, rows, 0:1]) * (1.0 / FULL)
            d = (
                up[rows, cols]
                + gain * scale * (dn_own[i, rows, :] + dn[1, i, rows, :].astype(f32))
                - xs[1][core, rows, cols].astype(f32) * (scale * scale * scale * cross)
            )
            delta[0, rows, cols] = (d * dgelu[0, rows, cols]).astype(bf)

        loop(LIVE // 64, dx)
    for k in (0, 1):
        begin(ring, k, nrm_t, delta)
    for k in (3, 0, 1):
        ring.forward(k, 0)
    order = (2, 3, 0, 1)
    for k in order:
        ring.finish(k, 0)
    for k in order:
        ring.forward(k, 1)
    for k in order:
        ring.finish(k, 1)
    for k in order:
        ring.last(k, grads)
    ring.wait_sends()
    scatter.wait_sends()
    for cp in (*swap_x, swap_logit, swap_stat, *swap_dn):
        cp.wait_send()


def hand_over(grads, loss, grads_out, loss_out, grads_held, loss_held, sem):
    into = [
        pltpu.make_async_copy(loss, loss_held, sem.at[0]),
        pltpu.make_async_copy(grads, grads_held, sem.at[1]),
    ]
    out = [
        pltpu.make_async_copy(loss_held, loss_out, sem.at[2]),
        pltpu.make_async_copy(grads_held, grads_out, sem.at[3]),
    ]
    for cp in into:
        cp.start()
    for a, b in zip(into, out):
        a.wait()
        b.start()
    for cp in out:
        cp.wait()


def body(features, gains, weights, heads, lengths, owners, labels):
    slots = features.shape[0]
    leaves, tree = flat([ring_scratch(), scatter_scratch(), work_scratch()])
    vmem, hbm = pl.BlockSpec(memory_space=pltpu.VMEM), pl.BlockSpec(memory_space=pl.ANY)
    grads, loss = pl.pallas_call(
        functools.partial(mega_kernel, tree),
        out_shape=(
            jax.ShapeDtypeStruct((2, 32, HALF), jnp.float32),
            jax.ShapeDtypeStruct((slots // 128, 128), jnp.bfloat16),
        ),
        in_specs=[hbm] * 7,
        out_specs=(vmem, vmem),
        scratch_shapes=leaves,
        compiler_params=pltpu.CompilerParams(
            collective_id=0, has_side_effects=True, vmem_limit_bytes=67043328
        ),
        name="step",
    )(
        features,
        gains,
        weights,
        heads.reshape(4, 4, 4, 2, 16, HALF),
        lengths,
        owners,
        labels.reshape(1, slots),
    )
    shapes = [jax.ShapeDtypeStruct(v.shape, v.dtype) for v in (grads, loss)]
    grads, loss = pl.pallas_call(
        hand_over,
        out_shape=shapes,
        in_specs=[hbm] * 2,
        out_specs=[hbm] * 2,
        scratch_shapes=[*[pltpu.VMEM(v.shape, v.dtype) for v in shapes], pltpu.SemaphoreType.DMA((4,))],
        name="hand_over",
    )(grads, loss)
    return (grads, loss.reshape(slots))


def solution(mesh):
    return jax.shard_map(
        body,
        mesh=mesh,
        in_specs=(
            P("dp", "mp"),
            P(),
            P(None, None, "mp"),
            P("dp", None, "mp"),
            P("dp", None),
            P("dp", None),
            P("dp"),
        ),
        out_specs=(P(None, "dp", "mp"), P("dp")),
        check_vma=False,
    )
```

```python
import functools
import math

import jax
import jax.numpy as jnp
from jax import lax
from jax.experimental import pallas as pl
from jax.experimental.pallas import tpu as pltpu
from jax.sharding import PartitionSpec as P

EPSILON = 1e-06
MESH = pl.DeviceIdType.MESH
STRIDES = (16, 4, 1)
WIDTHS = ((384, 256, 384), (384, 384, 256))
STARTS = tuple(tuple(sum(w[:k]) for k in range(3)) for w in WIDTHS)
UNITS = (16, 4, 1)
DIRECT = ()

def blend(core, a, b):
    return a + core * (b - a)

class Ring:
    def __init__(self, me, core, bufs):
        self.me, self.core = me, core
        self.g, self.t1, self.t2, self.rx, self.tx, self.ssem, self.rsem = bufs
        self.coords = tuple((me // s) % 4 for s in STRIDES)

    def place(self, c, ph):
        k0, k1 = (c + ph) % 3, (c + ph + 1) % 3
        stride = blend(self.core, STRIDES[k0], STRIDES[k1])
        return blend(self.core, self.coords[k0], self.coords[k1]), stride

    def dim(self, c, ph):
        p, stride = self.place(c, ph)
        right = self.me + ((p + 1) % 4 - p) * stride
        left = self.me + ((p + 3) % 4 - p) * stride
        return p, right, left

    def copies(self, k, c, ph):
        p, right, left = self.dim(c, ph)
        n = k * 3 + c
        part = (self.g, self.t1, self.t2)[ph][n]
        half = UNITS[ph] // 2
        lo, hi = pl.ds(0, half), pl.ds(half, half)

        def nth(i):
            if self.direct(k, ph):
                q = (p + (2, 1, 3)[i]) % 4
                src, to = part.at[q], self.me + (q - p) * self.place(c, ph)[1]
            elif i < 4:
                src = part.at[(p + (2, 1, 2, 3)[i]) % 4, (lo, hi, hi, lo)[i]]
                to = (right, right, left, left)[i]
            else:
                src = self.tx[ph][n].at[i - 4]
                to = (right, left)[i - 4]
            return pltpu.make_async_remote_copy(
                src_ref=src,
                dst_ref=self.rx[ph][n].at[i],
                send_sem=self.ssem.at[n, ph, i],
                recv_sem=self.rsem.at[n, ph, i],
                device_id=(to, self.core),
                device_id_type=MESH,
            )

        return nth

    @staticmethod
    def direct(k, ph):
        return ph == 2 or ph == 1 and k in DIRECT

    def start(self, k, c, ph):
        cp = self.copies(k, c, ph)
        for i in (0, 1, 2) if self.direct(k, ph) else (0, 2, 1, 3):
            cp(i).start()

    def forward(self, k, ph):
        half = UNITS[ph] // 2
        if self.direct(k, ph):
            return
        for c in range(3):
            n = k * 3 + c
            cp = self.copies(k, c, ph)
            p, _, _ = self.dim(c, ph)
            part, rx, tx = (self.g, self.t1)[ph][n], self.rx[ph][n], self.tx[ph][n]
            for i, q, off in ((0, (p + 1) % 4, 0), (2, (p + 3) % 4, half)):
                cp(i).wait_recv()

                def add(u, m):
                    tx[i // 2, pl.ds(u, m)] = (
                        part[q, pl.ds(off + u, m)].astype(jnp.float32)
                        + rx[i, pl.ds(u, m)].astype(jnp.float32)
                    ).astype(jnp.bfloat16)

                self.each(half, add)
                cp(4 + i // 2).start()

    def finish(self, k, ph):
        half, per = UNITS[ph] // 2, UNITS[ph + 1]
        for c in range(3):
            n = k * 3 + c
            cp = self.copies(k, c, ph)
            p, _, _ = self.dim(c, ph)
            part, rx, t = (self.g, self.t1)[ph][n], self.rx[ph][n], (self.t1, self.t2)[ph][n]
            if self.direct(k, ph):
                for i in range(3):
                    cp(i).wait_recv()
                for q in range(4):
                    v = part[p, q].astype(jnp.float32)
                    for i in range(3):
                        v = v + rx[i, q].astype(jnp.float32)
                    t[q, 0] = v.astype(jnp.bfloat16)
                self.start(k, c, ph + 1)
                continue
            for a, b, off in ((3, 4, 0), (1, 5, half)):
                cp(a).wait_recv()
                cp(b).wait_recv()

                def add(u, m):
                    v = (
                        part[p, pl.ds(off + u, m)].astype(jnp.float32)
                        + rx[a, pl.ds(u, m)].astype(jnp.float32)
                        + rx[b, pl.ds(u, m)].astype(jnp.float32)
                    ).astype(jnp.bfloat16)
                    for q in range(m // per):
                        t[(off + u) // per + q] = v[q * per : (q + 1) * per]

                self.each(half, add)
            self.start(k, c, ph + 1)

    def last(self, k, out):
        l, r = k // 2, k % 2
        for c in range(3):
            n = k * 3 + c
            cp = self.copies(k, c, 2)
            p, _, _ = self.dim(c, 2)
            for i in range(3):
                cp(i).wait_recv()
            total = self.t2[n][p, 0].astype(jnp.float32)
            for i in range(3):
                total = total + self.rx[2][n][i, 0].astype(jnp.float32)
            w0, w = STARTS[l][c], WIDTHS[l][c]
            out[l, 16 * r : 16 * r + 16, w0 : w0 + w] = total

    @staticmethod
    def each(count, f):
        n = min(count, 4)
        if count == n:
            f(0, n)
        else:

            def go(i, carry):
                f(pl.multiple_of(i * n, n), n)
                return carry

            lax.fori_loop(0, count // n, go, 0)

    def wait_sends(self):
        for k in range(4):
            for c in range(3):
                for ph in range(3):
                    for i in range(3 if self.direct(k, ph) else 6):
                        self.copies(k, c, ph)(i).wait_send()


def ring_scratch():
    bf = jnp.bfloat16
    streams = [(k, WIDTHS[k // 2][c]) for k in range(4) for c in range(3)]

    def arrive(k, w, ph):
        n = UNITS[ph]
        return (3, n, 16, w) if Ring.direct(k, ph) else (6, n // 2, 16, w)

    return [
        *[[pltpu.VMEM((4, n, 16, w), bf) for _, w in streams] for n in UNITS],
        [[pltpu.VMEM(arrive(k, w, ph), bf) for k, w in streams] for ph in range(3)],
        [[pltpu.VMEM((2, n // 2, 16, w), bf) for _, w in streams] for n in UNITS[:2]],
        pltpu.SemaphoreType.DMA((12, 3, 6)),
        pltpu.SemaphoreType.DMA((12, 3, 6)),
    ]


def flat(tree):
    return jax.tree.flatten(tree, is_leaf=lambda v: not isinstance(v, list))


def begin(ring, k, nt_ref, delta_ref):
    l, r = k // 2, k % 2
    for c in range(3):
        w0, w = STARTS[l][c], WIDTHS[l][c]
        g = ring.g[k * 3 + c]

        def group(x, carry):
            rows = pl.ds(pl.multiple_of(x * 256, 256), 256)
            prod = jnp.dot(
                nt_ref[l, r, rows, :], delta_ref[l, :, w0 : w0 + w], preferred_element_type=jnp.float32
            )
            v = prod.astype(jnp.bfloat16).reshape(16, 16, w)
            for i in range(16):
                xyz = (x, i // 4, i % 4)
                a, b, d = (
                    blend(ring.core, xyz[(c + e) % 3], xyz[(c + e + 1) % 3]) for e in range(3)
                )
                g[a, b * 4 + d] = v[i]
            return carry

        lax.fori_loop(0, 4, group, 0)
        ring.start(k, c, 0)


class Scatter:
    def __init__(self, ring, heads, bufs):
        self.ring, self.core, self.heads = ring, ring.core, heads
        self.r, self.ssem, self.rsem, self.lsem = bufs

    def piece(self, n, ph, q, j, m):
        h, c = n // 3, n % 3
        if ph == 0:
            w0, w = STARTS[h][c], WIDTHS[h][c]
            at = [slice(None)] * 3
            at[(c + m) % 3] = q
            at[(c + m + 1) % 3] = j
            return self.heads.at[(*at, h, slice(None), pl.ds(w0, w))]
        if ph == 1:
            return self.r[0][n].at[q, :, j]
        return self.r[1][n].at[q, j]

    def place(self, n, ph, j, s):
        return self.r[2][n].at[s, j] if ph == 2 else self.r[ph][n].at[j, s]

    def remote(self, n, ph, k, src, dst, to):
        return pltpu.make_async_remote_copy(
            src_ref=src,
            dst_ref=dst,
            send_sem=self.ssem.at[n, ph, k],
            recv_sem=self.rsem.at[n, ph, k],
            device_id=(to, self.core),
            device_id_type=MESH,
        )

    def on_core(self, ph, f):
        if ph:
            f(0)
        else:
            for m in range(2):
                pl.when(self.core == m)(functools.partial(f, m))

    def start(self, h, ph):
        def go(m):
            for j in range(4):
                for c in range(3):
                    n = h * 3 + c
                    p, stride = self.ring.place(c, ph)
                    for k in range(3):
                        q = (p + (2, 1, 3)[k]) % 4
                        self.remote(
                            n, ph, k, self.piece(n, ph, q, j, m), self.place(n, ph, j, p),
                            self.ring.me + (q - p) * stride,
                        ).start()
            for c in range(3):
                n = h * 3 + c
                p, _ = self.ring.place(c, ph)
                for j in range(4):
                    pltpu.make_async_copy(
                        self.piece(n, ph, p, j, m), self.place(n, ph, j, p), self.lsem.at[n, ph]
                    ).start()

        self.on_core(ph, go)

    def wait(self, n, ph, sem):
        ref = self.r[ph][n].at[0]
        pltpu.make_async_copy(ref, ref, sem).wait()

    def finish(self, h, ph):
        for c in range(3):
            n = h * 3 + c
            self.wait(n, ph, self.lsem.at[n, ph])
            for k in range(3):
                self.wait(n, ph, self.rsem.at[n, ph, k])

    def wait_sends(self):
        for n in range(6):
            for ph in range(3):
                for k in range(3):
                    self.wait(n, ph, self.ssem.at[n, ph, k])

    def owners_of(self, c):
        return tuple(
            blend(self.core, STRIDES[(c + k) % 3], STRIDES[(c + k + 1) % 3]) for k in range(3)
        )


def scatter_scratch():
    hc = [(h, c) for h in range(2) for c in range(3)]
    bf = jnp.bfloat16
    return [
        [[pltpu.VMEM((4, 4, 4, 16, WIDTHS[h][c]), bf) for h, c in hc] for _ in range(3)],
        pltpu.SemaphoreType.DMA((6, 3, 3)),
        pltpu.SemaphoreType.DMA((6, 3, 3)),
        pltpu.SemaphoreType.DMA((6, 3)),
    ]


LIVE = 256
HALF = 1024
FULL = 2048
C0 = math.sqrt(2 / math.pi)
C1 = 0.044715


def work_scratch():
    f32, bf = jnp.float32, jnp.bfloat16
    return [
        pltpu.VMEM((2, FULL, HALF), bf),
        [pltpu.VMEM((2, LIVE, HALF), bf) for _ in range(2)],
        pltpu.VMEM((LIVE, HALF), bf),
        pltpu.VMEM((LIVE, FULL), bf),
        pltpu.VMEM((2, 2, HALF, LIVE), bf),
        pltpu.VMEM((LIVE, 128), f32),
        pltpu.VMEM((2, LIVE, HALF), f32),
        pltpu.VMEM((LIVE, HALF), f32),
        pltpu.VMEM((LIVE, HALF), f32),
        pltpu.VMEM((2, LIVE, HALF), bf),
        pltpu.VMEM((2, 32, LIVE), f32),
        pltpu.VMEM((LIVE, 128), f32),
        pltpu.VMEM((LIVE, HALF), bf),
        pltpu.VMEM((2, LIVE, 128), f32),
        pltpu.VMEM((2, 4, LIVE, 256), bf),
        pltpu.VMEM((4, LIVE, 256), f32),
        pltpu.VMEM((2, FULL), f32),
        pltpu.VMEM((1, 64), jnp.int32),
        pltpu.VMEM((1, 64), jnp.int32),
        pltpu.VMEM((1, 2 * LIVE), jnp.int32),
        pltpu.SemaphoreType.DMA((8,)),
        pltpu.SemaphoreType.DMA((8,)),
        pltpu.SemaphoreType.DMA((8,)),
    ]


def loop(count, f):
    def go(i, carry):
        f(i)
        return carry

    lax.fori_loop(0, count, go, 0)


def mega_kernel(tree, feats, gains_hbm, weights, heads, lengths_hbm, owners_hbm, labels_hbm, grads, loss, *refs):
    me, core = lax.axis_index("dp"), lax.axis_index("mp")
    ring_bufs, scatter_bufs, work = jax.tree.unflatten(tree, refs)
    (wts, xs, x2, nrm, nrm_t, r1, dgelu, pre1, up, delta, logit, owner_down, spread, stat, dn, dn_own, gains, lengths, owners, labels, lsem, ssem, rsem) = work
    ring = Ring(me, core, ring_bufs)
    scatter = Scatter(ring, heads, scatter_bufs)
    other = 1 - core
    f32, bf = jnp.float32, jnp.bfloat16

    load = [pltpu.make_async_copy(weights.at[l], wts.at[l], lsem.at[l]) for l in range(2)]
    own_x = pltpu.make_async_copy(feats.at[pl.ds(0, LIVE)], xs[0].at[core], lsem.at[2])
    small = [
        pltpu.make_async_copy(src, dst, lsem.at[3 + i])
        for i, (src, dst) in enumerate(
            ((gains_hbm, gains), (lengths_hbm, lengths), (owners_hbm, owners), (labels_hbm, labels))
        )
    ]
    for cp in (own_x, *small, *load):
        cp.start()

    def swap(k, src, dst):
        return pltpu.make_async_remote_copy(
            src_ref=src,
            dst_ref=dst,
            send_sem=ssem.at[k],
            recv_sem=rsem.at[k],
            device_id=(me, other),
            device_id_type=MESH,
        )

    bar = pltpu.get_barrier_semaphore()
    pl.semaphore_signal(bar, inc=1, device_id=(me, other), device_id_type=MESH)
    for s in STRIDES:
        p = (me // s) % 4
        for step in (1, 2, 3):
            to = me + ((p + step) % 4 - p) * s
            pl.semaphore_signal(bar, inc=1, device_id=(to, core), device_id_type=MESH)
    pl.semaphore_wait(bar, 10)

    swap_x = [swap(0, feats.at[pl.ds(0, LIVE)], xs[0].at[core]), swap(1, xs[1].at[core], xs[1].at[core])]
    swap_x[0].start()
    for h in range(2):
        scatter.start(h, 0)

    def down(row):
        same = lax.broadcasted_iota(jnp.int32, (64, 64), 0) == lax.broadcasted_iota(jnp.int32, (64, 64), 1)
        return jnp.sum(jnp.where(same, row, 0), 1, keepdims=True)

    for cp in small:
        cp.wait()
    lens = lengths[...]
    upto = lax.broadcasted_iota(jnp.int32, (64, 64), 1) <= lax.broadcasted_iota(jnp.int32, (64, 64), 0)
    ends = jnp.sum(jnp.where(upto, lens, 0), 1, keepdims=True)
    lens_down = down(lens)
    slot = lax.broadcasted_iota(jnp.int32, (64, LIVE), 1)
    here = (slot < ends) & (slot >= ends - lens_down)
    slot_owner = jnp.sum(jnp.where(here, down(owners[...]), 0), 0, keepdims=True)
    slot_len = jnp.sum(jnp.where(here, lens_down, 0), 0, keepdims=True)
    owner_down[...] = jnp.broadcast_to(slot_owner.astype(f32), (128, LIVE)).T

    def norm_layer(l):
        def norm(i):
            rows = pl.ds(pl.multiple_of(i * 32, 32), 32)
            a, b = xs[l][0, rows, :].astype(f32), xs[l][1, rows, :].astype(f32)
            mean = (jnp.sum(a * a, -1, keepdims=True) + jnp.sum(b * b, -1, keepdims=True)) * (1.0 / FULL)
            scale = lax.rsqrt(mean + EPSILON)
            nrm[rows, 0:HALF] = (a * scale * gains[l : l + 1, 0:HALF]).astype(bf)
            nrm[rows, HALF:FULL] = (b * scale * gains[l : l + 1, HALF:FULL]).astype(bf)
            if l == 1:
                r1[rows, :] = jnp.broadcast_to(scale, (32, 128))

        loop(LIVE // 32, norm)

    def main_layer(l):
        def columns(i):
            cols = pl.ds(pl.multiple_of(i * 256, 256), 256)
            pre = jnp.dot(nrm[...], wts[l, :, cols], preferred_element_type=f32)
            t = jnp.tanh(C0 * (pre + C1 * (pre * pre * pre)))
            half = 0.5 * (1.0 + t)
            dgelu[l, :, cols] = half + 0.5 * pre * (1.0 - t * t) * (C0 * (1.0 + 3.0 * C1 * (pre * pre)))
            out = (xs[l][core, :, cols].astype(f32) + pre * half).astype(bf)
            if l == 0:
                xs[1][core, :, cols] = out
            else:
                x2[:, cols] = out
                pre1[:, cols] = pre

        loop(HALF // 256, columns)
        if l == 0:
            swap_x[1].start()

    def turn_layer(l):
        def turn(i):
            cols = pl.ds(pl.multiple_of(i * 256, 256), 256)
            turned = nrm[:, cols].astype(f32).T.astype(bf).reshape(8, 2, 16, LIVE)
            for k in range(2):
                nrm_t[l, k, pl.ds(pl.multiple_of(i * 128, 128), 128), :] = turned[:, k].reshape(128, LIVE)

        loop(FULL // 256, turn)

    own_x.wait()
    swap_x[0].wait_recv()
    norm_layer(0)
    load[0].wait()
    main_layer(0)
    turn_layer(0)
    scatter.finish(0, 0)
    scatter.start(0, 1)
    swap_x[1].wait_recv()
    norm_layer(1)
    load[1].wait()
    main_layer(1)
    scatter.finish(1, 0)
    scatter.start(1, 1)
    turn_layer(1)
    for h in range(2):
        scatter.finish(h, 1)
        scatter.start(h, 2)

    for h in range(2):
        scatter.finish(h, 2)
        total = jnp.zeros((16, LIVE), f32)
        for c in range(3):
            w0, w = STARTS[h][c], WIDTHS[h][c]
            sa, sb, sc = scatter.owners_of(c)
            block = scatter.r[2][h * 3 + c]

            prod = lax.dot_general(
                block[...].reshape(1024, w),
                x2[:, w0 : w0 + w],
                (((1,), (1,)), ((), ())),
                preferred_element_type=f32,
            )
            for k in range(64):
                owner = (k % 4) * sa + (k // 4 % 4) * sb + (k // 16) * sc
                total = total + jnp.where(slot_owner == owner, prod[k * 16 : k * 16 + 16], 0.0)
        logit[0, 16 * h : 16 * h + 16, :] = total
    swap_logit = swap(2, logit.at[0], logit.at[1])
    swap_logit.start()
    swap_logit.wait_recv()
    scores = logit[0] + logit[1]
    hit = lax.broadcasted_iota(jnp.int32, (32, LIVE), 0) == labels[0:1, 0:LIVE]
    log_total = jnp.log(jnp.sum(jnp.exp(scores), 0, keepdims=True))
    picked = jnp.sum(jnp.where(hit, scores, 0.0), 0, keepdims=True)
    losses = (log_total - picked).astype(bf)
    loss[0:1, :] = losses[:, 0:128]
    loss[1:2, :] = losses[:, 128:LIVE]
    loss[2:4, :] = jnp.zeros((2, 128), bf)
    dlogits = (jnp.exp(scores - log_total) - hit.astype(f32)) * (1.0 / slot_len.astype(f32))

    group = lax.broadcasted_iota(jnp.int32, (1, 128), 1) // 16
    for h in range(2):
        tiled = jnp.concatenate([dlogits[16 * h : 16 * h + 16]] * 8, axis=0).T
        for c in range(3):
            w0, w = STARTS[h][c], WIDTHS[h][c]
            sa, sb, sc = scatter.owners_of(c)
            for j in range(8):
                owner = (group % 4) * sa + (2 * (j % 2) + group // 4) * sb + (j // 2) * sc
                spread[:, 128 * j : 128 * j + 128] = jnp.where(
                    owner_down[...] == owner.astype(f32), tiled, 0.0
                ).astype(bf)
            block = scatter.r[2][h * 3 + c]
            grad = jnp.dot(spread[...], block[...].reshape(1024, w), preferred_element_type=f32)
            cols = slice(w0, w0 + w)
            up[:, cols] = grad if h == 0 else up[:, cols] + grad

    def back(i):
        rows = pl.ds(pl.multiple_of(i * 32, 32), 32)
        u = up[rows, :].astype(bf).astype(f32)
        up[rows, :] = u
        d = (u * dgelu[1, rows, :]).astype(bf)
        delta[1, rows, :] = d
        row = jnp.sum(d.astype(f32) * pre1[rows, :], -1, keepdims=True)
        stat[0, rows, :] = jnp.broadcast_to(row, (32, 128)) / r1[rows, :]

    loop(LIVE // 32, back)
    swap_stat = swap(3, stat.at[0], stat.at[1])
    swap_stat.start()

    for k in (2, 3):
        begin(ring, k, nrm_t, delta)
    swap_dn = [swap(4 + i, dn.at[0, i], dn.at[1, i]) for i in range(4)]
    for i in range(4):
        part = wts[1, pl.ds(pl.multiple_of(other * HALF + i * 256, 256), 256), :]
        dn[0, i] = lax.dot_general(
            delta[1], part, (((1,), (1,)), ((), ())), preferred_element_type=f32
        ).astype(bf)
        swap_dn[i].start()
    ring.forward(2, 0)

    def own_part(i):
        part = wts[1, pl.ds(pl.multiple_of(core * HALF + i * 256, 256), 256), :]
        dn_own[i] = lax.dot_general(delta[1], part, (((1,), (1,)), ((), ())), preferred_element_type=f32)

    loop(4, own_part)
    swap_stat.wait_recv()
    for i in range(4):
        swap_dn[i].wait_recv()
        cols = slice(256 * i, 256 * i + 256)
        gain = jnp.where(core == 0, gains[1:2, 256 * i : 256 * i + 256], gains[1:2, HALF + 256 * i : HALF + 256 * i + 256])

        def dx(k):
            rows = pl.ds(pl.multiple_of(k * 64, 64), 64)
            scale = r1[rows, 0:1]
            cross = (stat[0, rows, 0:1] + stat[1, rows, 0:1]) * (1.0 / FULL)
            d = (
                up[rows, cols]
                + gain * scale * (dn_own[i, rows, :] + dn[1, i, rows, :].astype(f32))
                - xs[1][core, rows, cols].astype(f32) * (scale * scale * scale * cross)
            )
            delta[0, rows, cols] = (d * dgelu[0, rows, cols]).astype(bf)

        loop(LIVE // 64, dx)
    for k in (0, 1):
        begin(ring, k, nrm_t, delta)
    for k in (3, 0, 1):
        ring.forward(k, 0)
    order = (2, 3, 0, 1)
    for k in order:
        ring.finish(k, 0)
    for k in order:
        ring.forward(k, 1)
    for k in order:
        ring.finish(k, 1)
    for k in order:
        ring.last(k, grads)
    ring.wait_sends()
    scatter.wait_sends()
    for cp in (*swap_x, swap_logit, swap_stat, *swap_dn):
        cp.wait_send()


def hand_over(grads, loss, grads_out, loss_out, grads_held, loss_held, sem):
    into = [
        pltpu.make_async_copy(loss, loss_held, sem.at[0]),
        pltpu.make_async_copy(grads, grads_held, sem.at[1]),
    ]
    out = [
        pltpu.make_async_copy(loss_held, loss_out, sem.at[2]),
        pltpu.make_async_copy(grads_held, grads_out, sem.at[3]),
    ]
    for cp in into:
        cp.start()
    for a, b in zip(into, out):
        a.wait()
        b.start()
    for cp in out:
        cp.wait()


def body(features, gains, weights, heads, lengths, owners, labels):
    slots = features.shape[0]
    leaves, tree = flat([ring_scratch(), scatter_scratch(), work_scratch()])
    vmem, hbm = pl.BlockSpec(memory_space=pltpu.VMEM), pl.BlockSpec(memory_space=pl.ANY)
    grads, loss = pl.pallas_call(
        functools.partial(mega_kernel, tree),
        out_shape=(
            jax.ShapeDtypeStruct((2, 32, HALF), jnp.float32),
            jax.ShapeDtypeStruct((slots // 128, 128), jnp.bfloat16),
        ),
        in_specs=[hbm] * 7,
        out_specs=(vmem, vmem),
        scratch_shapes=leaves,
        compiler_params=pltpu.CompilerParams(
            collective_id=0, has_side_effects=True, vmem_limit_bytes=67043328
        ),
        name="step",
    )(
        features,
        gains,
        weights,
        heads.reshape(4, 4, 4, 2, 16, HALF),
        lengths,
        owners,
        labels.reshape(1, slots),
    )
    shapes = [jax.ShapeDtypeStruct(v.shape, v.dtype) for v in (grads, loss)]
    grads, loss = pl.pallas_call(
        hand_over,
        out_shape=shapes,
        in_specs=[hbm] * 2,
        out_specs=[hbm] * 2,
        scratch_shapes=[*[pltpu.VMEM(v.shape, v.dtype) for v in shapes], pltpu.SemaphoreType.DMA((4,))],
        name="hand_over",
    )(grads, loss)
    return (grads, loss.reshape(slots))


def solution(mesh):
    return jax.shard_map(
        body,
        mesh=mesh,
        in_specs=(
            P("dp", "mp"),
            P(),
            P(None, None, "mp"),
            P("dp", None, "mp"),
            P("dp", None),
            P("dp", None),
            P("dp"),
        ),
        out_specs=(P(None, "dp", "mp"), P("dp")),
        check_vma=False,
    )
```

```python
import functools
import math

import jax
import jax.numpy as jnp
from jax import lax
from jax.experimental import pallas as pl
from jax.experimental.pallas import tpu as pltpu
from jax.sharding import PartitionSpec as P

EPSILON = 1e-06
MESH = pl.DeviceIdType.MESH
STRIDES = (16, 4, 1)
WIDTHS = ((384, 256, 384), (384, 384, 256))
STARTS = tuple(tuple(sum(w[:k]) for k in range(3)) for w in WIDTHS)
UNITS = (16, 4, 1)
DIRECT = ()

def blend(core, a, b):
    return a + core * (b - a)

class Ring:
    def __init__(self, me, core, bufs):
        self.me, self.core = me, core
        self.g, self.t1, self.t2, self.rx, self.tx, self.ssem, self.rsem = bufs
        self.coords = tuple((me // s) % 4 for s in STRIDES)

    def place(self, c, ph):
        k0, k1 = (c + ph) % 3, (c + ph + 1) % 3
        stride = blend(self.core, STRIDES[k0], STRIDES[k1])
        return blend(self.core, self.coords[k0], self.coords[k1]), stride

    def dim(self, c, ph):
        p, stride = self.place(c, ph)
        right = self.me + ((p + 1) % 4 - p) * stride
        left = self.me + ((p + 3) % 4 - p) * stride
        return p, right, left

    def copies(self, k, c, ph):
        p, right, left = self.dim(c, ph)
        n = k * 3 + c
        part = (self.g, self.t1, self.t2)[ph][n]
        half = UNITS[ph] // 2
        lo, hi = pl.ds(0, half), pl.ds(half, half)

        def nth(i):
            if self.direct(k, ph):
                q = (p + (2, 1, 3)[i]) % 4
                src, to = part.at[q], self.me + (q - p) * self.place(c, ph)[1]
            elif i < 4:
                src = part.at[(p + (2, 1, 2, 3)[i]) % 4, (lo, hi, hi, lo)[i]]
                to = (right, right, left, left)[i]
            else:
                src = self.tx[ph][n].at[i - 4]
                to = (right, left)[i - 4]
            return pltpu.make_async_remote_copy(
                src_ref=src,
                dst_ref=self.rx[ph][n].at[i],
                send_sem=self.ssem.at[n, ph, i],
                recv_sem=self.rsem.at[n, ph, i],
                device_id=(to, self.core),
                device_id_type=MESH,
            )

        return nth

    @staticmethod
    def direct(k, ph):
        return ph == 2 or ph == 1 and k in DIRECT

    def start(self, k, c, ph):
        cp = self.copies(k, c, ph)
        for i in (0, 1, 2) if self.direct(k, ph) else (0, 2, 1, 3):
            cp(i).start()

    def forward(self, k, ph):
        half = UNITS[ph] // 2
        if self.direct(k, ph):
            return
        for c in range(3):
            n = k * 3 + c
            cp = self.copies(k, c, ph)
            p, _, _ = self.dim(c, ph)
            part, rx, tx = (self.g, self.t1)[ph][n], self.rx[ph][n], self.tx[ph][n]
            for i, q, off in ((0, (p + 1) % 4, 0), (2, (p + 3) % 4, half)):
                cp(i).wait_recv()

                def add(u, m):
                    tx[i // 2, pl.ds(u, m)] = (
                        part[q, pl.ds(off + u, m)].astype(jnp.float32)
                        + rx[i, pl.ds(u, m)].astype(jnp.float32)
                    ).astype(jnp.bfloat16)

                self.each(half, add)
                cp(4 + i // 2).start()

    def finish(self, k, ph):
        half, per = UNITS[ph] // 2, UNITS[ph + 1]
        for c in range(3):
            n = k * 3 + c
            cp = self.copies(k, c, ph)
            p, _, _ = self.dim(c, ph)
            part, rx, t = (self.g, self.t1)[ph][n], self.rx[ph][n], (self.t1, self.t2)[ph][n]
            if self.direct(k, ph):
                for i in range(3):
                    cp(i).wait_recv()
                for q in range(4):
                    v = part[p, q].astype(jnp.float32)
                    for i in range(3):
                        v = v + rx[i, q].astype(jnp.float32)
                    t[q, 0] = v.astype(jnp.bfloat16)
                self.start(k, c, ph + 1)
                continue
            for a, b, off in ((3, 4, 0), (1, 5, half)):
                cp(a).wait_recv()
                cp(b).wait_recv()

                def add(u, m):
                    v = (
                        part[p, pl.ds(off + u, m)].astype(jnp.float32)
                        + rx[a, pl.ds(u, m)].astype(jnp.float32)
                        + rx[b, pl.ds(u, m)].astype(jnp.float32)
                    ).astype(jnp.bfloat16)
                    for q in range(m // per):
                        t[(off + u) // per + q] = v[q * per : (q + 1) * per]

                self.each(half, add)
            self.start(k, c, ph + 1)

    def last(self, k, out):
        l, r = k // 2, k % 2
        for c in range(3):
            n = k * 3 + c
            cp = self.copies(k, c, 2)
            p, _, _ = self.dim(c, 2)
            for i in range(3):
                cp(i).wait_recv()
            total = self.t2[n][p, 0].astype(jnp.float32)
            for i in range(3):
                total = total + self.rx[2][n][i, 0].astype(jnp.float32)
            w0, w = STARTS[l][c], WIDTHS[l][c]
            out[l, 16 * r : 16 * r + 16, w0 : w0 + w] = total

    @staticmethod
    def each(count, f):
        n = min(count, 4)
        if count == n:
            f(0, n)
        else:

            def go(i, carry):
                f(pl.multiple_of(i * n, n), n)
                return carry

            lax.fori_loop(0, count // n, go, 0)

    def wait_sends(self, ph):
        for k in range(4):
            for c in range(3):
                for i in range(3 if self.direct(k, ph) else 6):
                    self.copies(k, c, ph)(i).wait_send()


def ring_scratch():
    bf = jnp.bfloat16
    streams = [(k, WIDTHS[k // 2][c]) for k in range(4) for c in range(3)]

    def arrive(k, w, ph):
        n = UNITS[ph]
        return (3, n, 16, w) if Ring.direct(k, ph) else (6, n // 2, 16, w)

    return [
        *[[pltpu.VMEM((4, n, 16, w), bf) for _, w in streams] for n in UNITS],
        [[pltpu.VMEM(arrive(k, w, ph), bf) for k, w in streams] for ph in range(3)],
        [[pltpu.VMEM((2, n // 2, 16, w), bf) for _, w in streams] for n in UNITS[:2]],
        pltpu.SemaphoreType.DMA((12, 3, 6)),
        pltpu.SemaphoreType.DMA((12, 3, 6)),
    ]


def flat(tree):
    return jax.tree.flatten(tree, is_leaf=lambda v: not isinstance(v, list))


def begin(ring, k, nt_ref, delta_ref):
    l, r = k // 2, k % 2
    for c in range(3):
        w0, w = STARTS[l][c], WIDTHS[l][c]
        g = ring.g[k * 3 + c]

        def group(x, carry):
            rows = pl.ds(pl.multiple_of(x * 256, 256), 256)
            prod = jnp.dot(
                nt_ref[l, r, rows, :], delta_ref[l, :, w0 : w0 + w], preferred_element_type=jnp.float32
            )
            v = prod.astype(jnp.bfloat16).reshape(16, 16, w)
            for i in range(16):
                xyz = (x, i // 4, i % 4)
                a, b, d = (
                    blend(ring.core, xyz[(c + e) % 3], xyz[(c + e + 1) % 3]) for e in range(3)
                )
                g[a, b * 4 + d] = v[i]
            return carry

        lax.fori_loop(0, 4, group, 0)
        ring.start(k, c, 0)


class Scatter:
    def __init__(self, ring, heads, bufs):
        self.ring, self.core, self.heads = ring, ring.core, heads
        self.r, self.ssem, self.rsem, self.lsem = bufs

    def piece(self, n, ph, q, j, m):
        h, c = n // 3, n % 3
        if ph == 0:
            w0, w = STARTS[h][c], WIDTHS[h][c]
            at = [slice(None)] * 3
            at[(c + m) % 3] = q
            at[(c + m + 1) % 3] = j
            return self.heads.at[(*at, h, slice(None), pl.ds(w0, w))]
        if ph == 1:
            return self.r[0][n].at[q, :, j]
        return self.r[1][n].at[q, j]

    def place(self, n, ph, j, s):
        return self.r[2][n].at[s, j] if ph == 2 else self.r[ph][n].at[j, s]

    def remote(self, n, ph, k, src, dst, to):
        return pltpu.make_async_remote_copy(
            src_ref=src,
            dst_ref=dst,
            send_sem=self.ssem.at[n, ph, k],
            recv_sem=self.rsem.at[n, ph, k],
            device_id=(to, self.core),
            device_id_type=MESH,
        )

    def on_core(self, ph, f):
        if ph:
            f(0)
        else:
            for m in range(2):
                pl.when(self.core == m)(functools.partial(f, m))

    def start(self, h, ph):
        def go(m):
            for j in range(4):
                for c in range(3):
                    n = h * 3 + c
                    p, stride = self.ring.place(c, ph)
                    for k in range(3):
                        q = (p + (2, 1, 3)[k]) % 4
                        self.remote(
                            n, ph, k, self.piece(n, ph, q, j, m), self.place(n, ph, j, p),
                            self.ring.me + (q - p) * stride,
                        ).start()
            for c in range(3):
                n = h * 3 + c
                p, _ = self.ring.place(c, ph)
                for j in range(4):
                    pltpu.make_async_copy(
                        self.piece(n, ph, p, j, m), self.place(n, ph, j, p), self.lsem.at[n, ph]
                    ).start()

        self.on_core(ph, go)

    def wait(self, n, ph, sem):
        ref = self.r[ph][n].at[0]
        pltpu.make_async_copy(ref, ref, sem).wait()

    def finish(self, h, ph):
        for c in range(3):
            n = h * 3 + c
            self.wait(n, ph, self.lsem.at[n, ph])
            for k in range(3):
                self.wait(n, ph, self.rsem.at[n, ph, k])

    def wait_sends(self):
        for n in range(6):
            for ph in range(3):
                for k in range(3):
                    self.wait(n, ph, self.ssem.at[n, ph, k])

    def owners_of(self, c):
        return tuple(
            blend(self.core, STRIDES[(c + k) % 3], STRIDES[(c + k + 1) % 3]) for k in range(3)
        )


def scatter_scratch():
    hc = [(h, c) for h in range(2) for c in range(3)]
    bf = jnp.bfloat16
    return [
        [[pltpu.VMEM((4, 4, 4, 16, WIDTHS[h][c]), bf) for h, c in hc] for _ in range(3)],
        pltpu.SemaphoreType.DMA((6, 3, 3)),
        pltpu.SemaphoreType.DMA((6, 3, 3)),
        pltpu.SemaphoreType.DMA((6, 3)),
    ]


LIVE = 256
HALF = 1024
FULL = 2048
C0 = math.sqrt(2 / math.pi)
C1 = 0.044715


def work_scratch():
    f32, bf = jnp.float32, jnp.bfloat16
    return [
        pltpu.VMEM((2, FULL, HALF), bf),
        [pltpu.VMEM((2, LIVE, HALF), bf) for _ in range(2)],
        pltpu.VMEM((LIVE, HALF), bf),
        pltpu.VMEM((LIVE, FULL), bf),
        pltpu.VMEM((2, 2, HALF, LIVE), bf),
        pltpu.VMEM((LIVE, 128), f32),
        pltpu.VMEM((2, LIVE, HALF), f32),
        pltpu.VMEM((LIVE, HALF), f32),
        pltpu.VMEM((LIVE, HALF), f32),
        pltpu.VMEM((2, LIVE, HALF), bf),
        pltpu.VMEM((2, 32, LIVE), f32),
        pltpu.VMEM((LIVE, 128), bf),
        pltpu.VMEM((6, LIVE, HALF), bf),
        pltpu.VMEM((2, LIVE, 128), f32),
        pltpu.VMEM((2, 4, LIVE, 256), bf),
        pltpu.VMEM((4, LIVE, 256), f32),
        pltpu.VMEM((2, FULL), f32),
        pltpu.VMEM((1, 64), jnp.int32),
        pltpu.VMEM((1, 64), jnp.int32),
        pltpu.VMEM((1, 2 * LIVE), jnp.int32),
        pltpu.SemaphoreType.DMA((8,)),
        pltpu.SemaphoreType.DMA((8,)),
        pltpu.SemaphoreType.DMA((8,)),
    ]


def loop(count, f):
    def go(i, carry):
        f(i)
        return carry

    lax.fori_loop(0, count, go, 0)


def mega_kernel(tree, feats, gains_hbm, weights, heads, lengths_hbm, owners_hbm, labels_hbm, grads, loss, *refs):
    me, core = lax.axis_index("dp"), lax.axis_index("mp")
    ring_bufs, scatter_bufs, work = jax.tree.unflatten(tree, refs)
    (wts, xs, x2, nrm, nrm_t, r1, dgelu, pre1, up, delta, logit, owner_down, spread, stat, dn, dn_own, gains, lengths, owners, labels, lsem, ssem, rsem) = work
    ring = Ring(me, core, ring_bufs)
    scatter = Scatter(ring, heads, scatter_bufs)
    other = 1 - core
    f32, bf = jnp.float32, jnp.bfloat16

    load = [pltpu.make_async_copy(weights.at[l], wts.at[l], lsem.at[l]) for l in range(2)]
    own_x = pltpu.make_async_copy(feats.at[pl.ds(0, LIVE)], xs[0].at[core], lsem.at[2])
    small = [
        pltpu.make_async_copy(src, dst, lsem.at[3 + i])
        for i, (src, dst) in enumerate(
            ((gains_hbm, gains), (lengths_hbm, lengths), (owners_hbm, owners), (labels_hbm, labels))
        )
    ]
    for cp in (own_x, *small, *load):
        cp.start()

    def swap(k, src, dst):
        return pltpu.make_async_remote_copy(
            src_ref=src,
            dst_ref=dst,
            send_sem=ssem.at[k],
            recv_sem=rsem.at[k],
            device_id=(me, other),
            device_id_type=MESH,
        )

    bar = pltpu.get_barrier_semaphore()
    pl.semaphore_signal(bar, inc=1, device_id=(me, other), device_id_type=MESH)
    for s in STRIDES:
        p = (me // s) % 4
        for step in (1, 2, 3):
            to = me + ((p + step) % 4 - p) * s
            pl.semaphore_signal(bar, inc=1, device_id=(to, core), device_id_type=MESH)
    pl.semaphore_wait(bar, 10)

    swap_x = [swap(0, feats.at[pl.ds(0, LIVE)], xs[0].at[core]), swap(1, xs[1].at[core], xs[1].at[core])]
    swap_x[0].start()
    for h in range(2):
        scatter.start(h, 0)

    def down(row):
        same = lax.broadcasted_iota(jnp.int32, (64, 64), 0) == lax.broadcasted_iota(jnp.int32, (64, 64), 1)
        return jnp.sum(jnp.where(same, row, 0), 1, keepdims=True)

    for cp in small:
        cp.wait()
    lens = lengths[...]
    upto = lax.broadcasted_iota(jnp.int32, (64, 64), 1) <= lax.broadcasted_iota(jnp.int32, (64, 64), 0)
    ends = jnp.sum(jnp.where(upto, lens, 0), 1, keepdims=True)
    lens_down = down(lens)
    slot = lax.broadcasted_iota(jnp.int32, (64, LIVE), 1)
    here = (slot < ends) & (slot >= ends - lens_down)
    slot_owner = jnp.sum(jnp.where(here, down(owners[...]), 0), 0, keepdims=True)
    slot_len = jnp.sum(jnp.where(here, lens_down, 0), 0, keepdims=True)
    owner_down[...] = jnp.broadcast_to(slot_owner.astype(f32), (128, LIVE)).T.astype(bf)

    def norm_layer(l):
        def norm(i):
            rows = pl.ds(pl.multiple_of(i * 32, 32), 32)
            a, b = xs[l][0, rows, :].astype(f32), xs[l][1, rows, :].astype(f32)
            mean = (jnp.sum(a * a, -1, keepdims=True) + jnp.sum(b * b, -1, keepdims=True)) * (1.0 / FULL)
            scale = lax.rsqrt(mean + EPSILON)
            nrm[rows, 0:HALF] = (a * scale * gains[l : l + 1, 0:HALF]).astype(bf)
            nrm[rows, HALF:FULL] = (b * scale * gains[l : l + 1, HALF:FULL]).astype(bf)
            if l == 1:
                r1[rows, :] = jnp.broadcast_to(scale, (32, 128))

        loop(LIVE // 32, norm)

    def main_layer(l):
        def columns(i):
            cols = pl.ds(pl.multiple_of(i * 256, 256), 256)
            pre = jnp.dot(nrm[...], wts[l, :, cols], preferred_element_type=f32)
            t = jnp.tanh(C0 * (pre + C1 * (pre * pre * pre)))
            half = 0.5 * (1.0 + t)
            dgelu[l, :, cols] = half + 0.5 * pre * (1.0 - t * t) * (C0 * (1.0 + 3.0 * C1 * (pre * pre)))
            out = (xs[l][core, :, cols].astype(f32) + pre * half).astype(bf)
            if l == 0:
                xs[1][core, :, cols] = out
            else:
                x2[:, cols] = out
                pre1[:, cols] = pre

        loop(HALF // 256, columns)
        if l == 0:
            swap_x[1].start()

    def turn_layer(l):
        def turn(i):
            cols = pl.ds(pl.multiple_of(i * 256, 256), 256)
            turned = nrm[:, cols].astype(f32).T.astype(bf).reshape(8, 2, 16, LIVE)
            for k in range(2):
                nrm_t[l, k, pl.ds(pl.multiple_of(i * 128, 128), 128), :] = turned[:, k].reshape(128, LIVE)

        loop(FULL // 256, turn)

    own_x.wait()
    swap_x[0].wait_recv()
    norm_layer(0)
    load[0].wait()
    main_layer(0)
    turn_layer(0)
    scatter.finish(0, 0)
    scatter.start(0, 1)
    swap_x[1].wait_recv()
    norm_layer(1)
    load[1].wait()
    main_layer(1)
    scatter.finish(1, 0)
    scatter.start(1, 1)
    turn_layer(1)
    for h in range(2):
        scatter.finish(h, 1)
        scatter.start(h, 2)

    for h in range(2):
        scatter.finish(h, 2)
        total = jnp.zeros((16, LIVE), f32)
        for c in range(3):
            w0, w = STARTS[h][c], WIDTHS[h][c]
            sa, sb, sc = scatter.owners_of(c)
            block = scatter.r[2][h * 3 + c]

            prod = lax.dot_general(
                block[...].reshape(1024, w),
                x2[:, w0 : w0 + w],
                (((1,), (1,)), ((), ())),
                preferred_element_type=f32,
            )
            for k in range(64):
                owner = (k % 4) * sa + (k // 4 % 4) * sb + (k // 16) * sc
                total = total + jnp.where(slot_owner == owner, prod[k * 16 : k * 16 + 16], 0.0)
        logit[0, 16 * h : 16 * h + 16, :] = total
    swap_logit = swap(2, logit.at[0], logit.at[1])
    swap_logit.start()
    swap_logit.wait_recv()
    scores = logit[0] + logit[1]
    hit = lax.broadcasted_iota(jnp.int32, (32, LIVE), 0) == labels[0:1, 0:LIVE]
    log_total = jnp.log(jnp.sum(jnp.exp(scores), 0, keepdims=True))
    picked = jnp.sum(jnp.where(hit, scores, 0.0), 0, keepdims=True)
    losses = (log_total - picked).astype(bf)
    loss[0:1, :] = losses[:, 0:128]
    loss[1:2, :] = losses[:, 128:LIVE]
    loss[2:4, :] = jnp.zeros((2, 128), bf)
    dlogits = (jnp.exp(scores - log_total) - hit.astype(f32)) * (1.0 / slot_len.astype(f32))

    group = lax.broadcasted_iota(jnp.int32, (1, 128), 1) // 16
    for h in range(2):
        tiled = jnp.concatenate([dlogits[16 * h : 16 * h + 16]] * 8, axis=0).T.astype(bf)
        for c in range(3):
            w0, w = STARTS[h][c], WIDTHS[h][c]
            sa, sb, sc = scatter.owners_of(c)
            for j in range(8):
                owner = (group % 4) * sa + (2 * (j % 2) + group // 4) * sb + (j // 2) * sc
                spread[3 * h + c, :, 128 * j : 128 * j + 128] = jnp.where(
                    owner_down[...] == owner.astype(f32).astype(bf), tiled, jnp.zeros((), bf)
                )
            block = scatter.r[2][h * 3 + c]
            grad = jnp.dot(spread[3 * h + c], block[...].reshape(1024, w), preferred_element_type=f32)
            cols = slice(w0, w0 + w)
            up[:, cols] = grad if h == 0 else up[:, cols] + grad

    def back(i):
        rows = pl.ds(pl.multiple_of(i * 32, 32), 32)
        u = up[rows, :].astype(bf).astype(f32)
        up[rows, :] = u
        d = (u * dgelu[1, rows, :]).astype(bf)
        delta[1, rows, :] = d
        row = jnp.sum(d.astype(f32) * pre1[rows, :], -1, keepdims=True)
        stat[0, rows, :] = jnp.broadcast_to(row, (32, 128)) / r1[rows, :]

    loop(LIVE // 32, back)
    swap_stat = swap(3, stat.at[0], stat.at[1])
    swap_stat.start()

    for k in (2, 3):
        begin(ring, k, nrm_t, delta)
    swap_dn = [swap(4 + i, dn.at[0, i], dn.at[1, i]) for i in range(4)]
    for i in range(4):
        part = wts[1, pl.ds(pl.multiple_of(other * HALF + i * 256, 256), 256), :]
        dn[0, i] = lax.dot_general(
            delta[1], part, (((1,), (1,)), ((), ())), preferred_element_type=f32
        ).astype(bf)
        swap_dn[i].start()
    ring.forward(2, 0)

    def own_part(i):
        part = wts[1, pl.ds(pl.multiple_of(core * HALF + i * 256, 256), 256), :]
        dn_own[i] = lax.dot_general(delta[1], part, (((1,), (1,)), ((), ())), preferred_element_type=f32)

    loop(4, own_part)
    swap_stat.wait_recv()
    for i in range(4):
        swap_dn[i].wait_recv()
        cols = slice(256 * i, 256 * i + 256)
        gain = jnp.where(core == 0, gains[1:2, 256 * i : 256 * i + 256], gains[1:2, HALF + 256 * i : HALF + 256 * i + 256])

        def dx(k):
            rows = pl.ds(pl.multiple_of(k * 64, 64), 64)
            scale = r1[rows, 0:1]
            cross = (stat[0, rows, 0:1] + stat[1, rows, 0:1]) * (1.0 / FULL)
            d = (
                up[rows, cols]
                + gain * scale * (dn_own[i, rows, :] + dn[1, i, rows, :].astype(f32))
                - xs[1][core, rows, cols].astype(f32) * (scale * scale * scale * cross)
            )
            delta[0, rows, cols] = (d * dgelu[0, rows, cols]).astype(bf)

        loop(LIVE // 64, dx)
    for k in (0, 1):
        begin(ring, k, nrm_t, delta)
    for k in (3, 0):
        ring.forward(k, 0)
    scatter.wait_sends()
    for cp in (*swap_x, swap_logit, swap_stat, *swap_dn):
        cp.wait_send()
    ring.forward(1, 0)
    order = (2, 3, 0, 1)
    for k in order:
        ring.finish(k, 0)
    for k in order:
        ring.forward(k, 1)
    ring.wait_sends(0)
    for k in order:
        ring.finish(k, 1)
    ring.wait_sends(1)
    for k in order:
        ring.last(k, grads)
    ring.wait_sends(2)


def hand_over(grads, loss, grads_out, loss_out, grads_held, loss_held, sem):
    into = [
        pltpu.make_async_copy(loss, loss_held, sem.at[0]),
        pltpu.make_async_copy(grads, grads_held, sem.at[1]),
    ]
    out = [
        pltpu.make_async_copy(loss_held, loss_out, sem.at[2]),
        pltpu.make_async_copy(grads_held, grads_out, sem.at[3]),
    ]
    for cp in into:
        cp.start()
    for a, b in zip(into, out):
        a.wait()
        b.start()
    for cp in out:
        cp.wait()


def body(features, gains, weights, heads, lengths, owners, labels):
    slots = features.shape[0]
    leaves, tree = flat([ring_scratch(), scatter_scratch(), work_scratch()])
    vmem, hbm = pl.BlockSpec(memory_space=pltpu.VMEM), pl.BlockSpec(memory_space=pl.ANY)
    grads, loss = pl.pallas_call(
        functools.partial(mega_kernel, tree),
        out_shape=(
            jax.ShapeDtypeStruct((2, 32, HALF), jnp.float32),
            jax.ShapeDtypeStruct((slots // 128, 128), jnp.bfloat16),
        ),
        in_specs=[hbm] * 7,
        out_specs=(vmem, vmem),
        scratch_shapes=leaves,
        compiler_params=pltpu.CompilerParams(
            collective_id=0, has_side_effects=True, vmem_limit_bytes=67043328
        ),
        name="step",
    )(
        features,
        gains,
        weights,
        heads.reshape(4, 4, 4, 2, 16, HALF),
        lengths,
        owners,
        labels.reshape(1, slots),
    )
    shapes = [jax.ShapeDtypeStruct(v.shape, v.dtype) for v in (grads, loss)]
    grads, loss = pl.pallas_call(
        hand_over,
        out_shape=shapes,
        in_specs=[hbm] * 2,
        out_specs=[hbm] * 2,
        scratch_shapes=[*[pltpu.VMEM(v.shape, v.dtype) for v in shapes], pltpu.SemaphoreType.DMA((4,))],
        name="hand_over",
    )(grads, loss)
    return (grads, loss.reshape(slots))


def solution(mesh):
    return jax.shard_map(
        body,
        mesh=mesh,
        in_specs=(
            P("dp", "mp"),
            P(),
            P(None, None, "mp"),
            P("dp", None, "mp"),
            P("dp", None),
            P("dp", None),
            P("dp"),
        ),
        out_specs=(P(None, "dp", "mp"), P("dp")),
        check_vma=False,
    )
```
